32 devices in a mesh: region: 8 (over y, x, core), species: 4 (over z).
Axes of the slice: x: 2, y: 2, z: 4, core: 2. Of those that a mesh axis runs over, the one named last changes fastest.
Arguments:
- concentrations: float32 [256, 1024, 256], P('species', 'region'), may hold values from 0.05 to 5
- diffusion: float32 [256], P('species'), may hold values from 0.02 to 0.08
- courant_x: float32 [1024, 256], P('region'), may hold values from -0.2 to 0.2
- courant_y: float32 [1024, 256], P('region'), may hold values from -0.2 to 0.2
- log_rate: float32 [4, 768], replicated, may hold values from -3 to 0
- reactants: int32 [256, 768], replicated, may hold values from 0 to 1, as said below
- products: int32 [768, 256], replicated, may hold values from 0 to 1, as said below
- block_class: int32 [2048], P(('region', 'species')), may hold values from 0 to 3, as said below
- send_slot: int32 [2048], P(('region', 'species')), may hold values from -1 to 15, as said below
Outputs:
- reacted: float32 [256, 1024, 256], P('species', 'region')
The draws below stay inside these ranges and needn't reach their ends.
Inputs may be any that keep to these rules, and one draw needn't show every extreme that they name: `send_slot`: block n lies on the device with region index n // 256 and species index (n // 64) % 4. A value t >= 0 marks a stiff block and names slot t % 2 of region t // 2; -1 marks the others. Among the blocks of one species index every value from 0 to 15 occurs exactly once; for each species index one device holds exactly 8 marked blocks, and no device holds more. The marked blocks of one device name different regions. `block_class`: A block marked in send_slot has class 3; every other block has a lower class. `reactants`: every column has one or two ones, in different rows. `products`: every row has one or two ones, in different columns.
All inputs are finite; a program needn't handle non-finite values.
Results may differ from the reference program's by a relative error of at most 0.0003.
Values sent between devices are 32-bit elements; how exact they have to be, the bound alone decides.
A program may use at most 192 MiB of HBM per device.

```python
import math
import jax
import jax.numpy as jnp
from jax import lax

SPECIES = 256
REACT = 768
CX = 128
NY = 256
STEPS = 3
ITERS = 2
SUB = 2
CLASSES = 4
QUEUE = 2
STIFF_MOST = 8
NX = 1024
N_REGION = 8
N_SPECIES = 4


def stiff_plan(key):
    blocks_dev = CX * NY // (128 * N_SPECIES)
    total = N_REGION * QUEUE
    base = jax.random.fold_in(key, 7001)
    keys = jax.random.split(base, 5)
    heaviest = jax.random.randint(keys[0], (N_SPECIES,), 0, N_REGION)
    others = jax.random.randint(keys[1], (N_SPECIES, total), 0, N_REGION - 1)
    units = jnp.arange(total)
    region_of = jnp.where(units[None, :] < STIFF_MOST, heaviest[:, None], (heaviest[:, None] + 1 + others) % N_REGION)
    earlier = units[None, :, None] > units[None, None, :]
    same_region = region_of[:, :, None] == region_of[:, None, :]
    ranks = jnp.sum((same_region & earlier).astype(jnp.int32), axis=2)
    scores = jax.random.randint(keys[2], (N_SPECIES, N_REGION, blocks_dev), 0, 2 ** 20)
    orders = jnp.argsort(scores * blocks_dev + jnp.arange(blocks_dev), axis=-1).astype(jnp.int32)
    groups = jnp.broadcast_to(jnp.arange(N_SPECIES)[:, None], (N_SPECIES, total))
    block_of = orders[groups, region_of, ranks]
    sorted_units = jnp.argsort(region_of * total + units[None, :], axis=-1).astype(jnp.int32)
    position = jnp.argsort(sorted_units, axis=-1).astype(jnp.int32)
    rotation = jax.random.randint(keys[3], (N_SPECIES, 1), 0, N_REGION)
    label_scores = jax.random.randint(keys[4], (N_SPECIES, N_REGION), 0, 2 ** 20)
    labels = jnp.argsort(label_scores * N_REGION + jnp.arange(N_REGION)[None, :], axis=-1).astype(jnp.int32)
    target = jnp.take_along_axis(labels, (position + rotation) % N_REGION, axis=1)
    slot_of = (target * QUEUE + position // N_REGION).astype(jnp.int32)
    return (region_of, groups, block_of, slot_of)


def draw_send_slot(key, part):
    blocks_dev = CX * NY // (128 * N_SPECIES)
    region_of, groups, block_of, slot_of = stiff_plan(key)
    layout = jnp.full((N_REGION, N_SPECIES, blocks_dev), -1, jnp.int32)
    layout = layout.at[region_of, groups, block_of].set(slot_of)
    return layout.reshape(-1)


def draw_block_class(key, part):
    blocks_dev = CX * NY // (128 * N_SPECIES)
    region_of, groups, block_of, slot_of = stiff_plan(key)
    lower = jax.random.randint(jax.random.fold_in(key, 7002), (N_REGION, N_SPECIES, blocks_dev), 0, CLASSES - 1)
    layout = lower.at[region_of, groups, block_of].set(CLASSES - 1)
    return layout.reshape(-1).astype(jnp.int32)


def pair_table(key, salt):
    keys = jax.random.split(jax.random.fold_in(key, salt), 3)
    first_pick = jax.random.randint(keys[0], (REACT,), 0, SPECIES)
    offset = jax.random.randint(keys[1], (REACT,), 1, SPECIES)
    second_pick = (first_pick + offset) % SPECIES
    doubled = jax.random.randint(keys[2], (REACT,), 0, 2)
    species_ids = jnp.arange(SPECIES)[:, None]
    chosen = (species_ids == first_pick[None, :]) | (species_ids == second_pick[None, :]) & (doubled[None, :] == 1)
    return chosen.astype(jnp.int32)


def draw_reactants(key, part):
    return pair_table(key, 7101)


def draw_products(key, part):
    return pair_table(key, 7201).T


def block_levels(own_key, shape, cuts, low, largest):
    gain = 1.0
    for dim, parts in cuts:
        heights = jax.random.uniform(jax.random.fold_in(jax.random.fold_in(own_key, 6), dim), (parts,), jnp.float32, low / len(cuts), largest / len(cuts))
        gain = gain * jnp.repeat(jnp.exp(heights), shape[dim] // parts).reshape((-1,) + (1,) * (len(shape) - 1 - dim))
    return gain


def setup_inputs(seed: int = 0) -> dict:
    seeds = jax.random.split(jax.random.key(seed), 10)
    concentrations = jnp.clip(jnp.exp(math.log(5.0) - 4.6051702 * jax.random.uniform(seeds[0], (SPECIES, NX, NY), jnp.float32) ** block_levels(seeds[0], (SPECIES, NX, NY), ((0, 4), (1, 8)), -0.2, 0.2)), 0.05, 5.0)
    diffusion = jnp.clip(0.02 + 0.06 * jax.random.uniform(seeds[1], (SPECIES,), jnp.float32) ** block_levels(seeds[1], (SPECIES,), ((0, 4),), -0.2, 0.2), 0.02, 0.08)
    courant_x = jnp.clip(jax.random.uniform(seeds[2], (NX, NY), jnp.float32, -0.2, 0.2) * block_levels(seeds[2], (NX, NY), ((0, 8),), -0.4, 0.0), -0.2, 0.2)
    courant_y = jnp.clip(jax.random.uniform(seeds[3], (NX, NY), jnp.float32, -0.2, 0.2) * block_levels(seeds[3], (NX, NY), ((0, 8),), -0.4, 0.0), -0.2, 0.2)
    log_rate = jnp.clip(jax.random.uniform(seeds[4], (CLASSES, REACT), jnp.float32, -3.0, 0.0), -3.0, 0.0)
    reactants = draw_reactants(jax.random.fold_in(seeds[9], 71), 0)
    products = draw_products(jax.random.fold_in(seeds[9], 71), 0)
    block_class = draw_block_class(jax.random.fold_in(seeds[9], 71), 0)
    send_slot = draw_send_slot(jax.random.fold_in(seeds[9], 71), 0)
    return {"concentrations": concentrations, "diffusion": diffusion, "courant_x": courant_x, "courant_y": courant_y, "log_rate": log_rate, "reactants": reactants, "products": products, "block_class": block_class, "send_slot": send_slot}


floor_value = 0.05
highest = lax.Precision.HIGHEST


def minmod(first_diff, second):
    signed = jnp.sign(first_diff)
    return signed * jnp.maximum(0.0, jnp.minimum(jnp.abs(first_diff), signed * second))


def face_flux(field, courant, diffuse, axis_index):
    length = field.shape[axis_index]
    behind = lax.slice_in_dim(field, 0, length - 3, axis=axis_index)
    center = lax.slice_in_dim(field, 1, length - 2, axis=axis_index)
    forward = lax.slice_in_dim(field, 2, length - 1, axis=axis_index)
    beyond = lax.slice_in_dim(field, 3, length, axis=axis_index)
    upwind = center + 0.5 * (1.0 - courant) * minmod(center - behind, forward - center)
    downwind = forward - 0.5 * (1.0 + courant) * minmod(forward - center, beyond - forward)
    return courant * jnp.where(courant >= 0.0, upwind, downwind) - diffuse * (forward - center)


def substep(padded, wind_rows, cross_rows, diffuse):
    height = padded.shape[1]
    row_faces = 0.5 * (wind_rows[1:height - 2] + wind_rows[2:height - 1])
    flux_rows = face_flux(padded, row_faces[None], diffuse, 1)
    interior = padded[:, 2:height - 2]
    widened = jnp.pad(interior, ((0, 0), (0, 0), (2, 2)))
    cross_pad = jnp.pad(cross_rows, ((0, 0), (2, 2)))
    extent = cross_pad.shape[1]
    across = 0.5 * (cross_pad[:, 1:extent - 2] + cross_pad[:, 2:extent - 1])
    flux_cols = face_flux(widened, across[None], diffuse, 2)
    return interior - (flux_rows[:, 1:] - flux_rows[:, :-1]) - (flux_cols[:, :, 1:] - flux_cols[:, :, :-1])


def backward_euler(anchor, rate_logs, reactant_coef, product_coef, stride):
    iterate = anchor
    for iteration in range(ITERS):
        summed = lax.dot_general(reactant_coef, jnp.log(iterate), (((0,), (0,)), ((), ())), precision=highest, preferred_element_type=jnp.float32)
        reaction_rates = jnp.exp(rate_logs + summed)
        making = lax.dot_general(product_coef, reaction_rates, (((0,), (0,)), ((), ())), precision=highest, preferred_element_type=jnp.float32)
        losing = jnp.dot(reactant_coef, reaction_rates, precision=highest, preferred_element_type=jnp.float32)
        iterate = (anchor + stride * making) / (1.0 + stride * losing / iterate)
    return iterate


def stiff_steps(anchor, rate_logs, reactant_coef, product_coef):
    iterate = anchor
    for counter in range(SUB):
        iterate = backward_euler(iterate, rate_logs, reactant_coef, product_coef, 1.0 / SUB)
    return iterate


def reference(concentrations, diffusion, courant_x, courant_y, log_rate, reactants, products, block_class, send_slot):
    group_size = SPECIES // N_SPECIES
    wind_pad = jnp.pad(courant_x, ((2, 2), (0, 0)))

    def transport(pieces):
        concentration, spread = pieces
        diffuse = spread[:, None, None]
        for counter in range(STEPS):
            concentration = substep(jnp.pad(concentration, ((0, 0), (2, 2), (0, 0))), wind_pad, courant_y, diffuse)
        return concentration

    advected = lax.map(transport, (concentrations.reshape(N_SPECIES, group_size, NX, NY), diffusion.reshape(N_SPECIES, group_size)))
    piece_cells = CX * NY // N_SPECIES
    piece_count = NX * NY // piece_cells
    pieces_conc = advected.reshape(SPECIES, piece_count, piece_cells).transpose(1, 0, 2)
    cell_class = jnp.repeat(block_class, 128).reshape(piece_count, piece_cells)
    stiff_flags = jnp.repeat(send_slot >= 0, 128).reshape(piece_count, piece_cells)
    reactant_coef = reactants.astype(jnp.float32)
    product_coef = products.astype(jnp.float32)
    rate_table = log_rate.T

    def react(pieces):
        values, classes, flags = pieces
        anchor = jnp.maximum(values, floor_value)
        rate_logs = rate_table[:, classes]
        single_step = backward_euler(anchor, rate_logs, reactant_coef, product_coef, 1.0)
        multi_step = stiff_steps(anchor, rate_logs, reactant_coef, product_coef)
        return jnp.where(flags[None, :], multi_step, single_step)

    reacted = lax.map(react, (pieces_conc, cell_class, stiff_flags))
    return reacted.transpose(1, 0, 2).reshape(SPECIES, NX, NY)
```

```python
import functools

import jax
import jax.numpy as jnp
from jax import lax
from jax.experimental import pallas as pl
from jax.experimental.pallas import tpu as pltpu
from jax.sharding import PartitionSpec as P


STEPS = 3
ITERS = 2
SUB = 2
HALO = 2 * STEPS
BLOCK = 128
FLOOR = 0.05
LANES = 128
PAD = 8


def median0(p, r):
    return jnp.maximum(jnp.minimum(p, r), jnp.minimum(jnp.maximum(p, r), 0.0))


def next_column(vs, lane):
    r = [pltpu.roll(v, LANES - 1, 1) for v in vs] + [jnp.zeros_like(vs[0])]
    return [jnp.where(lane == LANES - 1, r[i + 1], r[i]) for i in range(len(vs))]


def previous_column(vs, lane):
    r = [jnp.zeros_like(vs[0])] + [pltpu.roll(v, 1, 1) for v in vs]
    return [jnp.where(lane == 0, r[i], r[i + 1]) for i in range(len(vs))]


def substep(src, dst, coef, nu, ahead, lo, groups, size):
    R = range(src.shape[2] // LANES)
    lane = lax.broadcasted_iota(jnp.int32, (8, LANES), 1)

    def col(v):
        return slice(v * LANES, (v + 1) * LANES)

    def ld(e):
        return [src[e, :, col(v)] for v in R]

    def c(e, k):
        whole = coef[e, pl.ds(k, 8, stride=0), :]
        return [whole[:, col(v)] for v in R]

    def right(e, k, q, s):
        a, b = c(e, k), c(e, k + 1)
        return [(a[v] + nu) * q[v] + b[v] * s[v] for v in R]

    def left(e, k, q, s):
        a, b = c(e, k), c(e, k + 1)
        return [(a[v] - nu) * q[v] + b[v] * s[v] for v in R]

    def minus(x, y):
        return [x[v] - y[v] for v in R]

    def plus(x, y):
        return [x[v] + y[v] for v in R]

    def slope(x, y):
        return [median0(x[v], y[v]) for v in R]

    def xstart(e):
        qb, qa, q0, q1 = ld(e - 2), ld(e - 1), ld(e), ld(e + 1)
        db, da, d0 = minus(qa, qb), minus(q0, qa), minus(q1, q0)
        sa, s0 = slope(db, da), slope(da, d0)
        f = plus(right(e - 1, 0, qa, sa), left(e, 2, q0, s0))
        return f, right(e, 0, q0, s0), d0, q1

    def xrow(e, carry):
        prev, out, d, q1 = carry
        q2 = ld(e + 2)
        d1 = minus(q2, q1)
        s = slope(d, d1)
        f = plus(out, left(e + 1, 2, q1, s))
        return minus(f, prev), (f, right(e + 1, 0, q1, s), d1, q2)

    def shift(t):
        for u in range(size):
            q = ld(lo + t * size + u)
            up, down = next_column(q, lane), previous_column(q, lane)
            for v in R:
                ahead[u, 0, :, col(v)] = up[v]
                ahead[u, 1, :, col(v)] = down[v]

    def update(t, carry):
        made = []
        for u in range(size):
            e = lo + t * size + u
            q = ld(e)
            up = [ahead[u, 0, :, col(v)] for v in R]
            down = [ahead[u, 1, :, col(v)] for v in R]
            s = slope(minus(q, down), minus(up, q))
            a, b = right(e, 4, q, s), left(e, 6, q, s)
            bn, ap = next_column(b, lane), previous_column(a, lane)
            div, carry = xrow(e, carry)
            made.append(minus(minus(minus(q, div), minus(a, b)), minus(bn, ap)))
        return made, carry

    def put(t, made):
        for u in range(size):
            for v in R:
                dst[lo + t * size + u, :, col(v)] = made[u][v]

    shift(0)

    def body(t, carry):
        made, carry = update(t - 1, carry)
        shift(t)
        put(t - 1, made)
        return carry

    carry = lax.fori_loop(1, groups, body, xstart(lo))
    made, _ = update(groups - 1, carry)
    put(groups - 1, made)


def transport_kernel(n, ids, x, top, bottom, nu_ref, coef, *rest):
    outs, (buf, other, ahead) = rest[:n], rest[n:]
    _, rows, cols = x.shape
    total = rows + 2 * PAD
    for r in range(HALO):
        buf[PAD - HALO + r] = top[:, r, :]
        buf[PAD + rows + r] = bottom[:, r, :]

    def turn(g, carry):
        at = pl.multiple_of(g * 8, 8)
        buf[pl.ds(PAD + at, 8)] = jnp.swapaxes(x[:, pl.ds(at, 8), :], 0, 1)
        return carry

    lax.fori_loop(0, rows // 8, turn, 0)
    nu = nu_ref[:, :LANES]
    zeros = jnp.zeros((PAD, 8, cols), jnp.float32)

    def clip(b):
        @pl.when(ids[1] == 0)
        def _():
            b[0:PAD] = zeros

        @pl.when(ids[1] == ids[2] - 1)
        def _():
            b[PAD + rows : total] = zeros

    count = rows // 16
    wide, size = (rows + 8) // count, 16
    substep(buf, other, coef, nu, ahead, PAD - 4, count, wide)
    clip(other)
    substep(other, buf, coef, nu, ahead, PAD - 4, count, wide)
    clip(buf)
    substep(buf, other, coef, nu, ahead, PAD, count, size)
    own = rows // n
    for s in range(n):
        owner = lax.rem(ids[0] + s, n)
        outs[s][...] = other[pl.ds(PAD + owner * own, own)]


def transport(ids, conc, top, bottom, nu, coef, n, chunk, offset):
    _, rows, cols = conc.shape
    own = rows // n
    base = offset // 8
    return pl.pallas_call(
        functools.partial(transport_kernel, n),
        grid_spec=pltpu.PrefetchScalarGridSpec(
            num_scalar_prefetch=1,
            grid=(chunk // 8,),
            in_specs=[
                pl.BlockSpec((8, rows, cols), lambda i, ids: (base + i, 0, 0)),
                pl.BlockSpec((8, HALO, cols), lambda i, ids: (base + i, 0, 0)),
                pl.BlockSpec((8, HALO, cols), lambda i, ids: (base + i, 0, 0)),
                pl.BlockSpec((8, cols), lambda i, ids: (base + i, 0)),
                pl.BlockSpec(coef.shape, lambda i, ids: (0, 0, 0)),
            ],
            out_specs=[pl.BlockSpec((own, 8, cols), lambda i, ids: (0, i, 0))] * n,
            scratch_shapes=[pltpu.VMEM((rows + 2 * PAD, 8, cols), jnp.float32)] * 2
            + [pltpu.VMEM(((rows + 8) // (rows // 16), 2, 8, cols), jnp.float32)],
        ),
        out_shape=[jax.ShapeDtypeStruct((own, chunk, cols), jnp.float32)] * n,
        compiler_params=pltpu.CompilerParams(vmem_limit_bytes=48 << 20),
        cost_estimate=pl.CostEstimate(
            flops=chunk * rows * cols * 160,
            bytes_accessed=chunk * rows * cols * 8,
            transcendentals=0,
        ),
    )(ids, conc, top, bottom, nu, coef)


def chemistry_kernel(n, parts, first, ordered, classes, slots, *rest):
    rest = rest[ordered:]
    pieces = rest[: n * parts]
    first_table, second_table, logs = rest[n * parts : n * parts + 3]
    outs = rest[n * parts + 3 : n * parts + 3 + n]
    anchor, state, lifted, rated, kept = rest[n * parts + 3 + n :]
    rows, _, cols = pieces[0].shape
    group = outs[0].shape[1]
    species = group * n
    sizes = [p.shape[1] for p in pieces]
    reactions = logs.shape[1]
    per_row = cols // BLOCK

    def iterate(lanes, stride):
        g = state[:, lanes]
        lg = jnp.log(g)
        hi = lg.astype(jnp.bfloat16)
        lifted[:species, lanes] = hi
        lifted[species:, lanes] = (lg - hi.astype(jnp.float32)).astype(jnp.bfloat16)
        summed = jnp.dot(first_table[...], lifted[:, lanes], preferred_element_type=jnp.float32)
        rate = jnp.exp(kept[:, lanes] + summed)
        hi = rate.astype(jnp.bfloat16)
        rated[:reactions, lanes] = hi
        rated[reactions:, lanes] = (rate - hi.astype(jnp.float32)).astype(jnp.bfloat16)
        both = jnp.dot(second_table[...], rated[:, lanes], preferred_element_type=jnp.float32)
        g = state[:, lanes]
        top = anchor[:, lanes] + stride * both[:species]
        state[:, lanes] = top / (1.0 + stride * both[species:] / g)

    whole = slice(0, cols)

    def one_row(r, carry):
        block = (first + pl.program_id(0) * rows + r) * per_row
        for b in range(per_row):
            kept[:, b * BLOCK : (b + 1) * BLOCK] = logs[classes[block + b]]
        for p in range(n * parts):
            start = jnp.maximum(pieces[p][r], FLOOR)
            at = sum(sizes[:p])
            anchor[at : at + sizes[p], :] = start
            state[at : at + sizes[p], :] = start

        def step(_, c):
            iterate(whole, 1.0)
            return c

        lax.fori_loop(0, ITERS, step, 0)
        for b in range(per_row):
            lanes = slice(b * BLOCK, (b + 1) * BLOCK)

            @pl.when(slots[block + b] >= 0)
            def _():
                state[:, lanes] = anchor[:, lanes]

                def sub(_, c):
                    anchor[:, lanes] = state[:, lanes]

                    def step(_, c2):
                        iterate(lanes, 1.0 / SUB)
                        return c2

                    return lax.fori_loop(0, ITERS, step, c)

                lax.fori_loop(0, SUB, sub, 0)

        for s in range(n):
            outs[s][r] = state[s * group : (s + 1) * group, :]
        return carry

    lax.fori_loop(0, rows, one_row, 0)


def chemistry(classes, slots, pieces, tables, logs, n, parts, first, count, step, previous):
    cols = pieces[0].shape[2]
    group = sum(p.shape[1] for p in pieces) // n
    ordered = [] if previous is None else [previous]
    species = group * n
    reactions = logs.shape[1]
    base = first // step

    def fixed(shape):
        return pl.BlockSpec(
            shape, lambda i, *_: (0,) * len(shape), pipeline_mode=pl.Buffered(1)
        )

    return pl.pallas_call(
        functools.partial(chemistry_kernel, n, parts, first, len(ordered)),
        grid_spec=pltpu.PrefetchScalarGridSpec(
            num_scalar_prefetch=2,
            grid=(count // step,),
            in_specs=[pl.BlockSpec(memory_space=pl.ANY)] * len(ordered)
            + [pl.BlockSpec((step, p.shape[1], cols), lambda i, *_: (base + i, 0, 0)) for p in pieces]
            + [fixed(tables[0].shape), fixed(tables[1].shape), fixed(logs.shape)],
            out_specs=[pl.BlockSpec((step, group, cols), lambda i, *_: (i, 0, 0))] * n,
            scratch_shapes=[
                pltpu.VMEM((species, cols), jnp.float32),
                pltpu.VMEM((species, cols), jnp.float32),
                pltpu.VMEM((2 * species, cols), jnp.bfloat16),
                pltpu.VMEM((2 * reactions, cols), jnp.bfloat16),
                pltpu.VMEM((reactions, cols), jnp.float32),
            ],
        ),
        out_shape=[jax.ShapeDtypeStruct((count, group, cols), jnp.float32)] * n,
        compiler_params=pltpu.CompilerParams(vmem_limit_bytes=48 << 20),
        cost_estimate=pl.CostEstimate(
            flops=count * cols * species * reactions * 2 * 6 * ITERS,
            bytes_accessed=count * cols * species * 8,
            transcendentals=count * cols * (species + reactions) * ITERS,
        ),
    )(classes, slots, *ordered, *pieces, *tables, logs)


def assemble_kernel(n, per, aliased, ids, *rest):
    pieces = rest[aliased : aliased + n * per]
    out = rest[-1]
    group = out.shape[0]
    at = pl.program_id(0)
    for s in range(n):

        @pl.when(at == s)
        def _():
            mine = pieces[s * per : (s + 1) * per]

            def turn(q, carry):
                sp = pl.ds(pl.multiple_of(q * 8, 8), 8)
                parts = [p[:, sp, :] for p in mine]
                v = parts[0] if per == 1 else jnp.concatenate(parts, axis=0)
                out[sp] = jnp.swapaxes(v, 0, 1)
                return carry

            lax.fori_loop(0, group // 8, turn, 0)


def assemble(ids, pieces, per, previous, shape, n, row):
    group, rows, cols = shape
    own = rows // n // 8
    aliased = 0 if previous is None else 1
    row_block = row // 8
    specs = [
        pl.BlockSpec(p.shape, lambda i, ids: (0, 0, 0), pipeline_mode=pl.Buffered(1))
        for p in pieces
    ]
    return pl.pallas_call(
        functools.partial(assemble_kernel, n, per, aliased),
        grid_spec=pltpu.PrefetchScalarGridSpec(
            num_scalar_prefetch=1,
            grid=(n,),
            in_specs=[pl.BlockSpec(memory_space=pl.ANY)] * aliased + specs,
            out_specs=pl.BlockSpec(
                (group, 8, cols), lambda i, ids: (0, lax.rem(ids[0] + i, n) * own + row_block, 0)
            ),
        ),
        out_shape=jax.ShapeDtypeStruct(shape, jnp.float32),
        input_output_aliases={1: 0} if aliased else {},
        compiler_params=pltpu.CompilerParams(vmem_limit_bytes=32 << 20),
        cost_estimate=pl.CostEstimate(
            flops=group * 8 * n * cols, bytes_accessed=group * 8 * n * cols * 8, transcendentals=0
        ),
    )(ids, *([previous] if aliased else []), *pieces)


def halo(conc, winds):
    devices = lax.axis_size("region")
    up = [(i, i + 1) for i in range(devices - 1)]
    down = [(j, i) for i, j in up]
    length = conc.shape[1]
    last = jnp.concatenate([conc[:, length - HALO :], winds[:, length - HALO :]], axis=0)
    leading = jnp.concatenate([conc[:, :HALO], winds[:, :HALO]], axis=0)
    return lax.ppermute(last, "region", up), lax.ppermute(leading, "region", down)


def face_coefficients(winds):
    cx, cy = winds[0], winds[1]
    ax = 0.5 * (cx + jnp.pad(cx[1:], ((0, 1), (0, 0))))
    before = jnp.pad(ax[:-1], ((1, 0), (0, 0)))
    ay = 0.5 * (cy + jnp.pad(cy[:, 1:], ((0, 0), (0, 1))))
    left = 0.5 * (cy + jnp.pad(cy[:, :-1], ((0, 0), (1, 0))))

    def ahead(a):
        p = jnp.maximum(a, 0.0)
        return [p, p * (0.5 * (1.0 - a))]

    def behind(a):
        m = jnp.minimum(a, 0.0)
        return [m, m * (-0.5 * (1.0 + a))]

    return jnp.stack(ahead(ax) + behind(before) + ahead(ay) + behind(left), axis=1)


def per_device(conc, diffusion, courant_x, courant_y, log_rate, reactants, products, block_class, send_slot):
    n = lax.axis_size("species")
    group, rows, cols = conc.shape
    me = lax.axis_index("species")
    region = lax.axis_index("region")
    ids = jnp.stack([me, region, jnp.int32(lax.axis_size("region"))]).astype(jnp.int32)
    own = rows // n
    sizes = [8, 8] + [16] * ((group - 16) // 16)
    parts = len(sizes)

    winds = jnp.stack([courant_x, courant_y])
    top, bottom = halo(conc, winds)
    winds = jnp.concatenate([top[group:], winds, bottom[group:]], axis=1)
    coef = face_coefficients(jnp.pad(winds, ((0, 0), (PAD - HALO, PAD - HALO), (0, 0))))
    nu = jnp.broadcast_to(diffusion[:, None], (group, cols))
    held = [[None] * parts for _ in range(n)]
    for j in range(parts):
        sent = transport(ids, conc, top, bottom, nu, coef, n, sizes[j], sum(sizes[:j]))
        held[0][j] = sent[0]
        for s in range(1, n):
            held[s][j] = lax.ppermute(sent[s], "species", [(i, (i + s) % n) for i in range(n)])

    order = lax.rem(me - jnp.arange(n) + n, n)
    reacts = jnp.take(reactants.reshape(n, group, -1), order, axis=0).reshape(n * group, -1)
    makes = jnp.take(products.T.reshape(n, group, -1), order, axis=0).reshape(n * group, -1)
    reacts, makes = reacts.astype(jnp.bfloat16), makes.astype(jnp.bfloat16)
    first_table = jnp.concatenate([reacts.T, reacts.T], axis=1)
    second = jnp.concatenate([makes, reacts], axis=0)
    second_table = jnp.concatenate([second, second], axis=1)
    logs = jnp.broadcast_to(log_rate[:, :, None], log_rate.shape + (BLOCK,))

    pieces = [held[s][j] for s in range(n) for j in range(parts)]
    step = 2
    counts = [2, 6] + [8] * (own // 8 - 1)
    result, at, waiting, made = None, 0, [], [None]
    for count in counts:
        made = chemistry(
            block_class, send_slot, pieces, (first_table, second_table), logs, n, parts, at, count, step, made[0]
        )
        back = [made[0]]
        for s in range(1, n):
            back.append(lax.ppermute(made[s], "species", [(i, (i - s) % n) for i in range(n)]))
        waiting.append(back)
        at += count
        if at % 8 == 0:
            done = [w[s] for s in range(n) for w in waiting]
            result = assemble(ids, done, len(waiting), result, conc.shape, n, at - 8)
            waiting = []
    return result


def solution(mesh):
    in_specs = (
        P("species", "region", None),
        P("species"),
        P("region", None),
        P("region", None),
        P(),
        P(),
        P(),
        P(("region", "species")),
        P(("region", "species")),
    )
    out_specs = P("species", "region", None)

    return jax.shard_map(per_device, mesh=mesh, in_specs=in_specs, out_specs=out_specs, check_vma=False)
```

```python
import functools

import jax
import jax.numpy as jnp
from jax import lax
from jax.experimental import pallas as pl
from jax.experimental.pallas import tpu as pltpu
from jax.sharding import PartitionSpec as P

STEPS = 3
ITERS = 2
SUB = 2
BLOCK = 128
FLOOR = 0.05
PAD = 8
GROUP = 8
ROWS = 16
MESH = pl.DeviceIdType.MESH


def median0(p, r):
    return jnp.maximum(jnp.minimum(p, r), jnp.minimum(jnp.maximum(p, r), 0.0))


def next_column(vs, lane):
    r = [pltpu.roll(v, BLOCK - 1, 1) for v in vs] + [jnp.zeros_like(vs[0])]
    return [jnp.where(lane == BLOCK - 1, r[i + 1], r[i]) for i in range(len(vs))]


def previous_column(vs, lane):
    r = [jnp.zeros_like(vs[0])] + [pltpu.roll(v, 1, 1) for v in vs]
    return [jnp.where(lane == 0, r[i], r[i + 1]) for i in range(len(vs))]


def substep(src, dst, coef, nu, ahead, lo, groups, size, base):
    R = range(src.shape[0])
    lane = lax.broadcasted_iota(jnp.int32, (8, BLOCK), 1)

    def ld(e):
        return [src[v, e] for v in R]

    def c(e, k):
        whole = coef[e, pl.ds(k, 8, stride=0), :]
        return [whole[:, v * BLOCK : (v + 1) * BLOCK] for v in R]

    def right(e, k, q, s):
        a, b = c(e, k), c(e, k + 1)
        return [(a[v] + nu) * q[v] + b[v] * s[v] for v in R]

    def left(e, k, q, s):
        a, b = c(e, k), c(e, k + 1)
        return [(a[v] - nu) * q[v] + b[v] * s[v] for v in R]

    def minus(x, y):
        return [x[v] - y[v] for v in R]

    def plus(x, y):
        return [x[v] + y[v] for v in R]

    def slope(x, y):
        return [median0(x[v], y[v]) for v in R]

    def xstart(e):
        qb, qa, q0, q1 = ld(e - 2), ld(e - 1), ld(e), ld(e + 1)
        db, da, d0 = minus(qa, qb), minus(q0, qa), minus(q1, q0)
        sa, s0 = slope(db, da), slope(da, d0)
        f = plus(right(e - 1, 0, qa, sa), left(e, 2, q0, s0))
        return f, right(e, 0, q0, s0), d0, q1

    def xrow(e, carry):
        prev, out, d, q1 = carry
        q2 = ld(e + 2)
        d1 = minus(q2, q1)
        s = slope(d, d1)
        f = plus(out, left(e + 1, 2, q1, s))
        return minus(f, prev), (f, right(e + 1, 0, q1, s), d1, q2)

    def shift(t):
        for u in range(size):
            q = ld(lo + t * size + u)
            up, down = next_column(q, lane), previous_column(q, lane)
            for v in R:
                ahead[u, 0, v] = up[v]
                ahead[u, 1, v] = down[v]

    def update(t, carry):
        made = []
        for u in range(size):
            e = lo + t * size + u
            q = ld(e)
            up = [ahead[u, 0, v] for v in R]
            down = [ahead[u, 1, v] for v in R]
            s = slope(minus(q, down), minus(up, q))
            a, b = right(e, 4, q, s), left(e, 6, q, s)
            bn, ap = next_column(b, lane), previous_column(a, lane)
            div, carry = xrow(e, carry)
            made.append(minus(minus(minus(q, div), minus(a, b)), minus(bn, ap)))
        return made, carry

    def put(t, made):
        for u in range(size):
            for v in R:
                dst[v, lo - base + t * size + u] = made[u][v]

    shift(0)

    def body(t, carry):
        made, carry = update(t - 1, carry)
        shift(t)
        put(t - 1, made)
        return carry

    carry = lax.fori_loop(1, groups, body, xstart(lo))
    made, _ = update(groups - 1, carry)
    put(groups - 1, made)


def next_lane(x, lane, cols):
    return jnp.where(lane == cols - 1, 0.0, pltpu.roll(x, cols - 1, 1))


def previous_lane(x, lane):
    return jnp.where(lane == 0, 0.0, pltpu.roll(x, 1, 1))


def face_coefficients(w, coef, total):
    cols = w.shape[2]
    lane = lax.broadcasted_iota(jnp.int32, (8, cols), 1)

    def ahead(a):
        p = jnp.maximum(a, 0.0)
        return [p, p * (0.5 * (1.0 - a))]

    def behind(a):
        m = jnp.minimum(a, 0.0)
        return [m, m * (-0.5 * (1.0 + a))]

    for e in range(0, total, 8):
        before, here, after = [w[0, e + 8 + k : e + 16 + k, :] for k in (-1, 0, 1)]
        cy = w[1, e + 8 : e + 16, :]
        ax, bx = 0.5 * (here + after), 0.5 * (before + here)
        ay, by = 0.5 * (cy + next_lane(cy, lane, cols)), 0.5 * (cy + previous_lane(cy, lane))
        kinds = jnp.stack(ahead(ax) + behind(bx) + ahead(ay) + behind(by), axis=0)
        coef[e : e + 8] = jnp.swapaxes(kinds, 0, 1)


def step_kernel(
    conc, cx, cy, nu_ref, log_rate, reactants, products, order, classes, slots, place,
    home, places,
    xin, top, bottom, winds, w, coef, buf, other, ahead, made, gathered, done,
    reacts, makes, first, second, logs, anchor, state, lifted, rated, kept,
    x_sem, t_sem, l_sem, halo_s, halo_r, wind_s, wind_r, out_s, out_r, home_s, home_r, place_s, place_r,
):
    n, nr = lax.axis_size("species"), lax.axis_size("region")
    me, region = lax.axis_index("species"), lax.axis_index("region")
    group, rows, cols = conc.shape
    halves = cols // BLOCK
    own = rows // n
    total = rows + 2 * PAD
    chunks = group // GROUP
    species = group * n
    reactions = log_rate.shape[1]
    blocks = own * halves
    not_first, not_last = region > 0, region < nr - 1

    def peer(j):
        up = 2 * me < n
        t = jnp.where(up, n - 1 - j - (n - 1 - j <= me).astype(jnp.int32), j + (j >= me).astype(jnp.int32))
        return t, lax.rem(t - me + n, n)

    def fetch(c):
        slot = lax.rem(c, 2)
        return pltpu.make_async_copy(conc.at[pl.ds(c * GROUP, GROUP)], xin.at[slot], x_sem.at[slot])

    def remote(src, dst, send, recv, where):
        return pltpu.make_async_remote_copy(
            src_ref=src, dst_ref=dst, send_sem=send, recv_sem=recv, device_id=where, device_id_type=MESH
        )

    barrier = pltpu.get_barrier_semaphore()
    for s in range(1, n):
        pl.semaphore_signal(barrier, inc=1, device_id={"species": lax.rem(me + s, n)}, device_id_type=MESH)

    @pl.when(not_first)
    def _():
        pl.semaphore_signal(barrier, inc=1, device_id={"region": region - 1}, device_id_type=MESH)

    @pl.when(not_last)
    def _():
        pl.semaphore_signal(barrier, inc=1, device_id={"region": region + 1}, device_id_type=MESH)

    fetch(0).start()
    w[...] = jnp.zeros_like(w)
    w[0, PAD + 8 : PAD + 8 + rows, :] = cx[...]
    w[1, PAD + 8 : PAD + 8 + rows, :] = cy[...]

    @pl.when(region == 0)
    def _():
        top[...] = jnp.zeros_like(top)

    @pl.when(region == nr - 1)
    def _():
        bottom[...] = jnp.zeros_like(bottom)

    pl.semaphore_wait(barrier, n - 1 + not_first.astype(jnp.int32) + not_last.astype(jnp.int32))

    ends = [(0, GROUP), (GROUP, group - GROUP)]

    def wind_copy(d, k):
        c = (cx, cy)[k]
        src = c.at[pl.ds(rows - 8, 8)] if d == 0 else c.at[pl.ds(0, 8)]
        to = region + 1 if d == 0 else region - 1
        return remote(src, winds.at[d, k], wind_s.at[d, k], wind_r.at[d, k], {"region": to})

    def halo_copy(d, piece):
        at, size = ends[piece]
        src = conc.at[pl.ds(at, size), pl.ds(rows - 8 if d == 0 else 0, 8)]
        dst = (top, bottom)[d].at[pl.ds(at, size)]
        to = region + 1 if d == 0 else region - 1
        return remote(src, dst, halo_s.at[d, piece], halo_r.at[d, piece], {"region": to})

    def send_edges(d):
        for k in range(2):
            wind_copy(d, k).start()
        for piece in range(2):
            halo_copy(d, piece).start()

    pl.when(not_last)(lambda: send_edges(0))
    pl.when(not_first)(lambda: send_edges(1))

    def place_copy(t, s, source):
        return remote(place, places.at[source], place_s.at[s], place_r.at[s], {"species": t})

    for j in range(n - 1):
        t, s = peer(j)
        place_copy(t, s, me).start()
    place_own = pltpu.make_async_copy(place, places.at[me], l_sem.at[0])
    place_own.start()
    take_reacts = pltpu.make_async_copy(reactants, reacts, t_sem.at[0])
    take_makes = pltpu.make_async_copy(products, makes, t_sem.at[1])
    take_reacts.start()
    take_makes.start()

    def take_winds(d):
        for k in range(2):
            wind_copy(d, k).wait_recv()
            at = 8 if d == 0 else 8 + PAD + rows
            w[k, at : at + 8, :] = winds[d, k]

    pl.when(not_first)(lambda: take_winds(0))
    pl.when(not_last)(lambda: take_winds(1))
    face_coefficients(w, coef, total)

    def clip(b):
        zeros = jnp.zeros((halves, PAD, GROUP, BLOCK), jnp.float32)

        @pl.when(region == 0)
        def _():
            b[:, 0:PAD] = zeros

        @pl.when(region == nr - 1)
        def _():
            b[:, PAD + rows : total] = zeros

    def take_halo(piece):
        pl.when(not_first)(lambda: halo_copy(0, piece).wait_recv())
        pl.when(not_last)(lambda: halo_copy(1, piece).wait_recv())

    def turn(value, at):
        moved = jnp.swapaxes(value, 0, 1)
        for v in range(halves):
            buf[v, pl.ds(at, 8)] = moved[:, :, v * BLOCK : (v + 1) * BLOCK]

    count = rows // ROWS

    def out_copy(c, t, s):
        return remote(
            made.at[c, :, pl.ds(t * own, own)],
            gathered.at[:, :, pl.ds(me * group + c * GROUP, GROUP), :],
            out_s.at[s], out_r.at[s], {"species": t},
        )

    def chunk(c, carry):
        fetch(c).wait()

        @pl.when(c + 1 < chunks)
        def _():
            fetch(c + 1).start()

        pl.when(c == 0)(lambda: take_halo(0))
        pl.when(c == 1)(lambda: take_halo(1))
        slot = lax.rem(c, 2)
        at = pl.multiple_of(c * GROUP, GROUP)
        turn(top[pl.ds(at, GROUP)], 0)
        turn(bottom[pl.ds(at, GROUP)], PAD + rows)

        def inner(g, carry):
            r = pl.multiple_of(g * 8, 8)
            turn(xin[slot, :, pl.ds(r, 8), :], PAD + r)
            return carry

        lax.fori_loop(0, rows // 8, inner, 0)
        nu = nu_ref[pl.ds(at, GROUP), :]
        wide = (rows + 8) // count
        substep(buf, other, coef, nu, ahead, PAD - 4, count, wide, 0)
        clip(other)
        substep(other, buf, coef, nu, ahead, PAD - 4, count, wide, 0)
        clip(buf)
        substep(buf, made.at[c], coef, nu, ahead, PAD, count, ROWS, PAD)
        for j in range(n - 1):
            t, s = peer(j)
            out_copy(c, t, s).start()
        mine = pl.ds(pl.multiple_of(me * group + c * GROUP, GROUP), GROUP)
        for v in range(halves):
            gathered[v, :, mine, :] = made[c, v, pl.ds(me * own, own)]
        return carry

    lax.fori_loop(0, chunks, chunk, 0)

    take_reacts.wait()
    take_makes.wait()
    for i in range(0, species, BLOCK):
        for j in range(0, reactions, BLOCK):
            ii, jj = slice(i, i + BLOCK), slice(j, j + BLOCK)
            uses = reacts[ii, jj].astype(jnp.float32)
            gives = makes[jj, ii].astype(jnp.float32)
            used, given = uses.T.astype(jnp.bfloat16), gives.T.astype(jnp.bfloat16)
            uses = uses.astype(jnp.bfloat16)
            first[jj, ii] = used
            first[jj, species + i : species + i + BLOCK] = used
            second[ii, jj] = given
            second[ii, reactions + j : reactions + j + BLOCK] = given
            second[species + i : species + i + BLOCK, jj] = uses
            second[species + i : species + i + BLOCK, reactions + j : reactions + j + BLOCK] = uses
    for k in range(log_rate.shape[0]):
        for j in range(0, reactions, BLOCK):
            row = jnp.broadcast_to(log_rate[k : k + 1, j : j + BLOCK], (BLOCK, BLOCK))
            logs[k, j : j + BLOCK, :] = row.T

    for s in range(1, n):
        source = lax.rem(me - s + n, n)
        part = gathered.at[:, :, pl.ds(source * group, group), :]
        remote(part, part, out_s.at[s], out_r.at[s], {"species": source}).wait_recv()

    lane = lax.broadcasted_iota(jnp.int32, (1, 2 * BLOCK), 1)

    def iterate(stride):
        lg = jnp.log(state[...])
        hi = lg.astype(jnp.bfloat16)
        lifted[:species] = hi
        lifted[species:] = (lg - hi.astype(jnp.float32)).astype(jnp.bfloat16)
        summed = jnp.dot(first[...], lifted[...], preferred_element_type=jnp.float32)
        rate = jnp.exp(kept[...] + summed)
        hi = rate.astype(jnp.bfloat16)
        rated[:reactions] = hi
        rated[reactions:] = (rate - hi.astype(jnp.float32)).astype(jnp.bfloat16)
        both = jnp.dot(second[...], rated[...], preferred_element_type=jnp.float32)
        state[...] = (anchor[...] + stride * both[:species]) / (1.0 + stride * both[species:] / state[...])

    slow = (blocks - min(nr, blocks)) // 2

    def home_copy(p, t, s):
        return remote(
            done.at[pl.ds(2 * p, 2), pl.ds(t * group, group), :],
            home.at[me, pl.ds(2 * p, 2)],
            home_s.at[s], home_r.at[s], {"species": t},
        )

    def pair(p, carry):
        where = [order[2 * p], order[2 * p + 1]]
        stiff = [slots[b] >= 0 for b in where]
        for k in range(2):
            lanes = slice(k * BLOCK, (k + 1) * BLOCK)
            b = where[k]
            value = jnp.maximum(gathered[lax.rem(b, halves), lax.div(b, halves)], FLOOR)
            anchor[:, lanes] = value
            state[:, lanes] = value
            kept[:, lanes] = logs[classes[b]]

        def advance(u, carry):
            other_stride = jnp.where(u == 0, 1.0, 0.0)
            left, right = [jnp.where(f, 1.0 / SUB, other_stride) for f in stiff]
            stride = jnp.where(lane < BLOCK, left, right)

            @pl.when(u > 0)
            def _():
                anchor[...] = state[...]

            def again(_, carry):
                iterate(stride)
                return carry

            return lax.fori_loop(0, ITERS, again, carry)

        lax.fori_loop(0, jnp.where(p >= slow, SUB, 1), advance, 0)
        for k in range(2):
            done[2 * p + k] = state[:, k * BLOCK : (k + 1) * BLOCK]
        for j in range(n - 1):
            t, s = peer(j)
            home_copy(p, t, s).start()
        return carry

    lax.fori_loop(0, blocks // 2, pair, 0)
    kept_home = pltpu.make_async_copy(done.at[:, pl.ds(me * group, group), :], home.at[me], l_sem.at[1])
    kept_home.start()

    def edges_sent(d):
        for k in range(2):
            wind_copy(d, k).wait_send()
        for piece in range(2):
            halo_copy(d, piece).wait_send()

    pl.when(not_last)(lambda: edges_sent(0))
    pl.when(not_first)(lambda: edges_sent(1))
    place_own.wait()
    kept_home.wait()
    for s in range(1, n):
        t, source = lax.rem(me + s, n), lax.rem(me - s + n, n)
        place_copy(t, s, me).wait_send()
        place_copy(t, s, source).wait_recv()
        sent = made.at[:, :, pl.ds(t * own, own)]
        remote(sent, sent, out_s.at[s], out_r.at[s], {"species": t}).wait_send()
        sent = done.at[:, pl.ds(t * group, group), :]
        remote(sent, home.at[me], home_s.at[s], home_r.at[s], {"species": t}).wait_send()
        remote(sent, home.at[source], home_s.at[s], home_r.at[s], {"species": t}).wait_recv()


def take_step(conc, courant_x, courant_y, nu, log_rate, reactants, products, order, classes, slots, place, n):
    group, rows, cols = conc.shape
    halves, own = cols // BLOCK, rows // n
    species, reactions = reactants.shape
    chunks, blocks = group // GROUP, own * halves
    total = rows + 2 * PAD
    wide = (rows + 8) // (rows // ROWS)
    f32, bf16 = jnp.float32, jnp.bfloat16
    V, D = pltpu.VMEM, pltpu.SemaphoreType.DMA
    vmem, smem, hbm = [pl.BlockSpec(memory_space=m) for m in (pltpu.VMEM, pltpu.SMEM, pl.ANY)]
    return pl.pallas_call(
        step_kernel,
        name="step",
        in_specs=[hbm, vmem, vmem, vmem, vmem, hbm, hbm, smem, smem, smem, vmem],
        out_specs=[hbm, hbm],
        out_shape=[
            jax.ShapeDtypeStruct((n, blocks, group, BLOCK), f32),
            jax.ShapeDtypeStruct((n,) + place.shape, jnp.int32),
        ],
        scratch_shapes=[
            V((2, GROUP, rows, cols), f32),
            V((group, 8, cols), f32),
            V((group, 8, cols), f32),
            V((2, 2, 8, cols), f32),
            V((2, total + 16, cols), f32),
            V((total, 8, cols), f32),
            V((halves, total, GROUP, BLOCK), f32),
            V((halves, total, GROUP, BLOCK), f32),
            V((wide, 2, halves, GROUP, BLOCK), f32),
            V((chunks, halves, rows, GROUP, BLOCK), f32),
            V((halves, own, species, BLOCK), f32),
            V((blocks, species, BLOCK), f32),
            V((species, reactions), jnp.int32),
            V((reactions, species), jnp.int32),
            V((reactions, 2 * species), bf16),
            V((2 * species, 2 * reactions), bf16),
            V((log_rate.shape[0], reactions, BLOCK), f32),
            V((species, 2 * BLOCK), f32),
            V((species, 2 * BLOCK), f32),
            V((2 * species, 2 * BLOCK), bf16),
            V((2 * reactions, 2 * BLOCK), bf16),
            V((reactions, 2 * BLOCK), f32),
            D((2,)), D((2,)), D((2,)),
            D((2, 2)), D((2, 2)), D((2, 2)), D((2, 2)),
            D((n,)), D((n,)), D((n,)), D((n,)), D((n,)), D((n,)),
        ],
        compiler_params=pltpu.CompilerParams(
            collective_id=0, has_side_effects=True, vmem_limit_bytes=60 << 20
        ),
    )(conc, courant_x, courant_y, nu, log_rate, reactants, products, order, classes, slots, place)


def assemble_kernel(halves, steps, place, home, out):
    group = out.shape[0]
    i = pl.program_id(0)
    source, row = lax.div(i, steps), lax.rem(i, steps) * 8

    where = [[place[source, 0, (row + j) * halves + v] for j in range(8)] for v in range(halves)]

    def turn(g, carry):
        sp = pl.ds(pl.multiple_of(g * 8, 8), 8)
        for v in range(halves):
            tiles = jnp.stack([home[0, where[v][j], sp, :] for j in range(8)], axis=0)
            out[sp, :, v * BLOCK : (v + 1) * BLOCK] = jnp.swapaxes(tiles, 0, 1)
        return carry

    lax.fori_loop(0, group // 8, turn, 0)


def assemble(places, home, shape):
    group, rows, cols = shape
    n, blocks = home.shape[:2]
    steps = rows // n // 8
    return pl.pallas_call(
        functools.partial(assemble_kernel, cols // BLOCK, steps),
        name="assemble",
        grid_spec=pltpu.PrefetchScalarGridSpec(
            num_scalar_prefetch=1,
            grid=(rows // 8,),
            in_specs=[pl.BlockSpec((1, blocks, group, BLOCK), lambda i, p: (lax.div(i, steps), 0, 0, 0))],
            out_specs=pl.BlockSpec((group, 8, cols), lambda i, p: (0, i, 0)),
        ),
        out_shape=jax.ShapeDtypeStruct(shape, jnp.float32),
        compiler_params=pltpu.CompilerParams(vmem_limit_bytes=32 << 20),
    )(places, home)


def per_device(conc, diffusion, courant_x, courant_y, log_rate, reactants, products, block_class, send_slot):
    n = lax.axis_size("species")
    blocks = send_slot.shape[0]
    number = jnp.arange(blocks, dtype=jnp.int32)
    key = number + jnp.where(send_slot >= 0, blocks, 0)
    place = jnp.sum((key[None, :] < key[:, None]).astype(jnp.int32), axis=1)
    order = jnp.sum(jnp.where(place[:, None] == number[None, :], number[:, None], 0), axis=0)
    place = jnp.broadcast_to(jnp.pad(place, (0, BLOCK - blocks))[None], (8, BLOCK))
    nu = jnp.broadcast_to(diffusion[:, None], (diffusion.shape[0], BLOCK))
    home, places = take_step(
        conc, courant_x, courant_y, nu, log_rate, reactants, products, order, block_class, send_slot, place, n
    )
    return assemble(places, home, conc.shape)


def solution(mesh):
    in_specs = (
        P("species", "region", None),
        P("species"),
        P("region", None),
        P("region", None),
        P(),
        P(),
        P(),
        P(("region", "species")),
        P(("region", "species")),
    )
    out_specs = P("species", "region", None)
    return jax.shard_map(per_device, mesh=mesh, in_specs=in_specs, out_specs=out_specs, check_vma=False)
```

```python
import functools

import jax
import jax.numpy as jnp
from jax import lax
from jax.experimental import pallas as pl
from jax.experimental.pallas import tpu as pltpu
from jax.sharding import PartitionSpec as P

STEPS = 3
ITERS = 2
SUB = 2
BLOCK = 128
FLOOR = 0.05
PAD = 8
GROUP = 8
WIDEST = 20
QUARTERS = 4
MESH = pl.DeviceIdType.MESH


def median0(p, r):
    return jnp.maximum(jnp.minimum(p, r), jnp.minimum(jnp.maximum(p, r), 0.0))


def next_column(vs, lane):
    r = [pltpu.roll(v, BLOCK - 1, 1) for v in vs] + [jnp.zeros_like(vs[0])]
    return [jnp.where(lane == BLOCK - 1, r[i + 1], r[i]) for i in range(len(vs))]


def previous_column(vs, lane):
    r = [jnp.zeros_like(vs[0])] + [pltpu.roll(v, 1, 1) for v in vs]
    return [jnp.where(lane == 0, r[i], r[i + 1]) for i in range(len(vs))]


def substep(src, dst, coef, nu, ahead, lo, groups, size, base):
    R = range(src.shape[0])
    lane = lax.broadcasted_iota(jnp.int32, (8, BLOCK), 1)

    def ld(e):
        return [src[v, e] for v in R]

    def c(e, k):
        whole = coef[e, pl.ds(k, 8, stride=0), :]
        return [whole[:, v * BLOCK : (v + 1) * BLOCK] for v in R]

    def right(e, k, q, s):
        a, b = c(e, k), c(e, k + 1)
        return [(a[v] + nu) * q[v] + b[v] * s[v] for v in R]

    def left(e, k, q, s):
        a, b = c(e, k), c(e, k + 1)
        return [(a[v] - nu) * q[v] + b[v] * s[v] for v in R]

    def minus(x, y):
        return [x[v] - y[v] for v in R]

    def plus(x, y):
        return [x[v] + y[v] for v in R]

    def slope(x, y):
        return [median0(x[v], y[v]) for v in R]

    def xstart(e):
        qb, qa, q0, q1 = ld(e - 2), ld(e - 1), ld(e), ld(e + 1)
        db, da, d0 = minus(qa, qb), minus(q0, qa), minus(q1, q0)
        sa, s0 = slope(db, da), slope(da, d0)
        f = plus(right(e - 1, 0, qa, sa), left(e, 2, q0, s0))
        return f, right(e, 0, q0, s0), d0, q1

    def xrow(e, carry):
        prev, out, d, q1 = carry
        q2 = ld(e + 2)
        d1 = minus(q2, q1)
        s = slope(d, d1)
        f = plus(out, left(e + 1, 2, q1, s))
        return minus(f, prev), (f, right(e + 1, 0, q1, s), d1, q2)

    def shift(t):
        for u in range(size):
            q = ld(lo + t * size + u)
            up, down = next_column(q, lane), previous_column(q, lane)
            for v in R:
                ahead[u, 0, v] = up[v]
                ahead[u, 1, v] = down[v]

    def update(t, carry):
        made = []
        for u in range(size):
            e = lo + t * size + u
            q = ld(e)
            up = [ahead[u, 0, v] for v in R]
            down = [ahead[u, 1, v] for v in R]
            s = slope(minus(q, down), minus(up, q))
            a, b = right(e, 4, q, s), left(e, 6, q, s)
            bn, ap = next_column(b, lane), previous_column(a, lane)
            div, carry = xrow(e, carry)
            made.append(minus(minus(minus(q, div), minus(a, b)), minus(bn, ap)))
        return made, carry

    def put(t, made):
        for u in range(size):
            for v in R:
                dst[v, lo - base + t * size + u] = made[u][v]

    shift(0)

    def body(t, carry):
        made, carry = update(t - 1, carry)
        shift(t)
        put(t - 1, made)
        return carry

    carry = lax.fori_loop(1, groups, body, xstart(lo))
    made, _ = update(groups - 1, carry)
    put(groups - 1, made)


def next_lane(x, lane, cols):
    return jnp.where(lane == cols - 1, 0.0, pltpu.roll(x, cols - 1, 1))


def previous_lane(x, lane):
    return jnp.where(lane == 0, 0.0, pltpu.roll(x, 1, 1))


def face_coefficients(w, coef, starts):
    cols = w.shape[2]
    lane = lax.broadcasted_iota(jnp.int32, (8, cols), 1)

    def ahead(a):
        p = jnp.maximum(a, 0.0)
        return [p, p * (0.5 * (1.0 - a))]

    def behind(a):
        m = jnp.minimum(a, 0.0)
        return [m, m * (-0.5 * (1.0 + a))]

    for e in starts:
        before, here, after = [w[0, e + 8 + k : e + 16 + k, :] for k in (-1, 0, 1)]
        cy = w[1, e + 8 : e + 16, :]
        ax, bx = 0.5 * (here + after), 0.5 * (before + here)
        ay, by = 0.5 * (cy + next_lane(cy, lane, cols)), 0.5 * (cy + previous_lane(cy, lane))
        kinds = jnp.stack(ahead(ax) + behind(bx) + ahead(ay) + behind(by), axis=0)
        coef[e : e + 8] = jnp.swapaxes(kinds, 0, 1)


def split(m):
    size = max(k for k in range(1, WIDEST + 1) if m % k == 0)
    return m // size, size


def step_kernel(
    conc, nus, cx, cy, log_rate, reactants, products, facts, tile,
    home, places,
    xin, top, bottom, winds, courant, w, coef, buf, other, third, ahead, low, middle, high, made, gathered, done,
    reacts, makes, rates, first, second, logs, anchor, state, lifted, rated, kept,
    x_sem, t_sem, c_sem, l_sem, halo_s, halo_r, wind_s, wind_r, first_s, out_s, out_r, home_s, home_r, place_s, place_r,
):
    n, nr = lax.axis_size("species"), lax.axis_size("region")
    me, region = lax.axis_index("species"), lax.axis_index("region")
    group, rows, cols = conc.shape
    halves = cols // BLOCK
    own = rows // n
    total = rows + 2 * PAD
    chunks = group // GROUP
    species = group * n
    reactions = log_rate.shape[1]
    blocks = own * halves
    not_first, not_last = region > 0, region < nr - 1

    def peer(j):
        up = 2 * me < n
        t = jnp.where(up, n - 1 - j - (n - 1 - j <= me).astype(jnp.int32), j + (j >= me).astype(jnp.int32))
        return t, lax.rem(t - me + n, n)

    def fetch(c):
        slot = lax.rem(c, 2)
        return pltpu.make_async_copy(conc.at[pl.ds(c * GROUP, GROUP)], xin.at[slot], x_sem.at[slot])

    def remote(src, dst, send, recv, where):
        return pltpu.make_async_remote_copy(
            src_ref=src, dst_ref=dst, send_sem=send, recv_sem=recv, device_id=where, device_id_type=MESH
        )

    barrier = pltpu.get_barrier_semaphore()
    for s in range(1, n):
        pl.semaphore_signal(barrier, inc=1, device_id={"species": lax.rem(me + s, n)}, device_id_type=MESH)

    @pl.when(not_first)
    def _():
        pl.semaphore_signal(barrier, inc=1, device_id={"region": region - 1}, device_id_type=MESH)

    @pl.when(not_last)
    def _():
        pl.semaphore_signal(barrier, inc=1, device_id={"region": region + 1}, device_id_type=MESH)

    fetch(0).start()
    take_courant = [pltpu.make_async_copy(c, courant.at[k], c_sem.at[k]) for k, c in enumerate((cx, cy))]
    take_small = [
        pltpu.make_async_copy(a, b, t_sem.at[k])
        for k, (a, b) in enumerate(
            [(log_rate, rates), (reactants, reacts), (products, makes)]
        )
    ]
    for copy in take_courant + take_small:
        copy.start()
    for at in (0, PAD + 8 + rows):
        w[:, at : at + PAD + 8, :] = jnp.zeros((2, PAD + 8, cols), jnp.float32)

    @pl.when(region == 0)
    def _():
        top[...] = jnp.zeros_like(top)

    @pl.when(region == nr - 1)
    def _():
        bottom[...] = jnp.zeros_like(bottom)

    for copy in take_courant:
        copy.wait()
    w[:, PAD + 8 : PAD + 8 + rows, :] = courant[...]
    face_coefficients(w, coef, range(0, total, 8))
    pl.semaphore_wait(barrier, n - 1 + not_first.astype(jnp.int32) + not_last.astype(jnp.int32))

    ends = [(0, GROUP), (GROUP, group - GROUP)]

    def wind_copy(d, k):
        c = (cx, cy)[k]
        src = c.at[pl.ds(rows - 8, 8)] if d == 0 else c.at[pl.ds(0, 8)]
        to = region + 1 if d == 0 else region - 1
        return remote(src, winds.at[d, k], wind_s.at[d, k], wind_r.at[d, k], {"region": to})

    def halo_copy(d, piece):
        at, size = ends[piece]
        src = conc.at[pl.ds(at, size), pl.ds(rows - 8 if d == 0 else 0, 8)]
        dst = (top, bottom)[d].at[pl.ds(at, size)]
        to = region + 1 if d == 0 else region - 1
        return remote(src, dst, halo_s.at[d, piece], halo_r.at[d, piece], {"region": to})

    def send_edges(d):
        for k in range(2):
            wind_copy(d, k).start()
        for piece in range(2):
            halo_copy(d, piece).start()

    pl.when(not_last)(lambda: send_edges(0))
    pl.when(not_first)(lambda: send_edges(1))

    def place_copy(t, s, source):
        return remote(tile, places.at[source], place_s.at[s], place_r.at[s], {"species": t})

    for j in range(n - 1):
        t, s = peer(j)
        place_copy(t, s, me).start()
    place_own = pltpu.make_async_copy(tile, places.at[me], l_sem.at[0])
    place_own.start()

    def take_winds(d):
        for k in range(2):
            wind_copy(d, k).wait_recv()
            at = 8 if d == 0 else 8 + PAD + rows
            w[k, at : at + 8, :] = winds[d, k]

    def clip(b):
        zeros = jnp.zeros((halves, PAD, GROUP, BLOCK), jnp.float32)

        @pl.when(region == 0)
        def _():
            b[:, 0:PAD] = zeros

        @pl.when(region == nr - 1)
        def _():
            b[:, PAD + rows : total] = zeros

    def take_halo(piece):
        pl.when(not_first)(lambda: halo_copy(0, piece).wait_recv())
        pl.when(not_last)(lambda: halo_copy(1, piece).wait_recv())

    def turn(value, at):
        moved = jnp.swapaxes(value, 0, 1)
        for v in range(halves):
            buf[v, pl.ds(at, 8)] = moved[:, :, v * BLOCK : (v + 1) * BLOCK]

    def out_copy(c, src, send, t, s):
        dst = gathered.at[:, :, pl.ds(me * group + c * GROUP, GROUP), :]
        return remote(src, dst, send.at[s], out_r.at[s], {"species": t})

    def arrive(c):
        fetch(c).wait()

        @pl.when(c + 1 < chunks)
        def _():
            fetch(c + 1).start()

        slot = lax.rem(c, 2)

        def inner(g, carry):
            r = pl.multiple_of(g * 8, 8)
            turn(xin[slot, :, pl.ds(r, 8), :], PAD + r)
            return carry

        lax.fori_loop(0, rows // 8, inner, 0)

    def arrive_halo(c):
        at = pl.multiple_of(c * GROUP, GROUP)
        turn(top[pl.ds(at, GROUP)], 0)
        turn(bottom[pl.ds(at, GROUP)], PAD + rows)

    def spread(c):
        sub = lax.broadcasted_iota(jnp.int32, (GROUP, BLOCK), 0)
        nu = jnp.zeros((GROUP, BLOCK), jnp.float32)
        for k in range(GROUP):
            nu = jnp.where(sub == k, nus[c * GROUP + k], nu)
        return nu

    def advance(dst, nu, lo, size, mid, edge):
        wide, few = split(size + 8), split(size)
        substep(buf, other, coef, nu, ahead, PAD + lo - 4, *wide, 0)
        if edge:
            clip(other)
        substep(other, mid, coef, nu, ahead, PAD + lo - 4, *wide, 0)
        if edge:
            clip(mid)
        substep(mid, dst, coef, nu, ahead, PAD + lo, *few, PAD + lo)

    def keep(c, src, row):
        mine = pl.ds(pl.multiple_of(me * group + c * GROUP, GROUP), GROUP)
        for v in range(halves):
            gathered[v, :, mine, :] = src[v, pl.ds(row, own)]

    def strip(src, lo, size):
        def holds(t):
            return (t * own >= lo) & (t * own < lo + size)

        for j in range(n - 1):
            t, s = peer(j)

            @pl.when(holds(t))
            def _():
                out_copy(0, src.at[:, pl.ds(t * own - lo, own)], first_s, t, s).start()

        @pl.when(holds(me))
        def _():
            keep(0, src, me * own - lo)

    arrive(0)
    nu = spread(0)
    if rows > 2 * own:
        advance(middle, nu, own, rows - 2 * own, third, False)
        strip(middle, own, rows - 2 * own)
    pl.when(not_first)(lambda: take_winds(0))
    pl.when(not_last)(lambda: take_winds(1))
    face_coefficients(w, coef, [0, 8, total - 16, total - 8])
    take_halo(0)
    arrive_halo(0)
    advance(low, nu, 0, own, third, True)
    strip(low, 0, own)
    advance(high, nu, rows - own, own, third, True)
    strip(high, rows - own, own)
    take_halo(1)

    def chunk(c, carry):
        arrive(c)
        arrive_halo(c)
        advance(made.at[c - 1], spread(c), 0, rows, buf, True)
        for j in range(n - 1):
            t, s = peer(j)
            out_copy(c, made.at[c - 1, :, pl.ds(t * own, own)], out_s, t, s).start()
        keep(c, made.at[c - 1], me * own)
        return carry

    lax.fori_loop(1, chunks, chunk, 0)

    for copy in take_small:
        copy.wait()
    for i in range(0, species, BLOCK):
        for j in range(0, reactions, BLOCK):
            ii, jj = slice(i, i + BLOCK), slice(j, j + BLOCK)
            uses = reacts[ii, jj].astype(jnp.float32)
            gives = makes[jj, ii].astype(jnp.float32)
            used, given = uses.T.astype(jnp.bfloat16), gives.T.astype(jnp.bfloat16)
            uses = uses.astype(jnp.bfloat16)
            first[jj, ii] = used
            first[jj, species + i : species + i + BLOCK] = used
            second[ii, jj] = given
            second[ii, reactions + j : reactions + j + BLOCK] = given
            second[species + i : species + i + BLOCK, jj] = uses
            second[species + i : species + i + BLOCK, reactions + j : reactions + j + BLOCK] = uses
    for k in range(log_rate.shape[0]):
        for j in range(0, reactions, BLOCK):
            row = jnp.broadcast_to(rates[k : k + 1, j : j + BLOCK], (BLOCK, BLOCK))
            logs[k, j : j + BLOCK, :] = row.T

    for s in range(1, n):
        source = lax.rem(me - s + n, n)
        part = gathered.at[:, :, pl.ds(source * group, group), :]
        remote(part, part, out_s.at[s], out_r.at[s], {"species": source}).wait_recv()

    lane = lax.broadcasted_iota(jnp.int32, (1, 2 * BLOCK), 1)

    def iterate(stride):
        lg = jnp.log(state[...])
        hi = lg.astype(jnp.bfloat16)
        lifted[:species] = hi
        lifted[species:] = (lg - hi.astype(jnp.float32)).astype(jnp.bfloat16)
        summed = jnp.dot(first[...], lifted[...], preferred_element_type=jnp.float32)
        rate = jnp.exp(kept[...] + summed)
        hi = rate.astype(jnp.bfloat16)
        rated[:reactions] = hi
        rated[reactions:] = (rate - hi.astype(jnp.float32)).astype(jnp.bfloat16)
        both = jnp.dot(second[...], rated[...], preferred_element_type=jnp.float32)
        state[...] = (anchor[...] + stride * both[:species]) / (1.0 + stride * both[species:] / state[...])

    slow = (blocks - min(nr, blocks)) // 2

    def home_copy(p, t, s):
        return remote(
            done.at[pl.ds(2 * p, 2), pl.ds(t * group, group), :],
            home.at[me, pl.ds(2 * p, 2)],
            home_s.at[s], home_r.at[s], {"species": t},
        )

    def pair(p, carry):
        where = [facts[2 * p], facts[2 * p + 1]]
        stiff = [facts[blocks + 2 * p + k] >= 0 for k in range(2)]
        for k in range(2):
            lanes = slice(k * BLOCK, (k + 1) * BLOCK)
            b = where[k]
            value = jnp.maximum(gathered[lax.rem(b, halves), lax.div(b, halves)], FLOOR)
            anchor[:, lanes] = value
            state[:, lanes] = value
            kept[:, lanes] = logs[facts[2 * blocks + 2 * p + k]]

        def again_from(u, carry):
            other_stride = jnp.where(u == 0, 1.0, 0.0)
            left, right = [jnp.where(f, 1.0 / SUB, other_stride) for f in stiff]
            stride = jnp.where(lane < BLOCK, left, right)

            @pl.when(u > 0)
            def _():
                anchor[...] = state[...]

            def again(_, carry):
                iterate(stride)
                return carry

            return lax.fori_loop(0, ITERS, again, carry)

        lax.fori_loop(0, jnp.where(p >= slow, SUB, 1), again_from, 0)
        for k in range(2):
            done[2 * p + k] = state[:, k * BLOCK : (k + 1) * BLOCK]
        for j in range(n - 1):
            t, s = peer(j)
            home_copy(p, t, s).start()
        return carry

    lax.fori_loop(0, blocks // 2, pair, 0)
    kept_home = pltpu.make_async_copy(done.at[:, pl.ds(me * group, group), :], home.at[me], l_sem.at[1])
    kept_home.start()

    def edges_sent(d):
        for k in range(2):
            wind_copy(d, k).wait_send()
        for piece in range(2):
            halo_copy(d, piece).wait_send()

    pl.when(not_last)(lambda: edges_sent(0))
    pl.when(not_first)(lambda: edges_sent(1))
    place_own.wait()
    kept_home.wait()
    for s in range(1, n):
        t, source = lax.rem(me + s, n), lax.rem(me - s + n, n)
        place_copy(t, s, me).wait_send()
        place_copy(t, s, source).wait_recv()
        remote(low, low, first_s.at[s], out_r.at[s], {"species": t}).wait_send()
        sent = made.at[:, :, pl.ds(t * own, own)]
        remote(sent, sent, out_s.at[s], out_r.at[s], {"species": t}).wait_send()
        sent = done.at[:, pl.ds(t * group, group), :]
        remote(sent, home.at[me], home_s.at[s], home_r.at[s], {"species": t}).wait_send()
        remote(sent, home.at[source], home_s.at[s], home_r.at[s], {"species": t}).wait_recv()


def take_step(conc, diffusion, courant_x, courant_y, log_rate, reactants, products, facts, place, n):
    group, rows, cols = conc.shape
    halves, own = cols // BLOCK, rows // n
    species, reactions = reactants.shape
    chunks, blocks = group // GROUP, own * halves
    total = rows + 2 * PAD
    f32, bf16, i32 = jnp.float32, jnp.bfloat16, jnp.int32
    V, D = pltpu.VMEM, pltpu.SemaphoreType.DMA
    whole = [pltpu.with_memory_space_constraint(a, pltpu.HBM) for a in (courant_x, courant_y, log_rate, reactants, products)]
    hbm, smem = pl.BlockSpec(memory_space=pltpu.HBM), pl.BlockSpec(memory_space=pltpu.SMEM)
    return pl.pallas_call(
        step_kernel,
        name="step",
        in_specs=[hbm, smem] + [hbm] * 5 + [smem, pl.BlockSpec(memory_space=pltpu.VMEM)],
        out_specs=[pl.BlockSpec(memory_space=pl.ANY)] * 2,
        out_shape=[
            jax.ShapeDtypeStruct((n, blocks, group, BLOCK), f32),
            jax.ShapeDtypeStruct((n, 8, BLOCK), i32),
        ],
        scratch_shapes=[
            V((2, GROUP, rows, cols), f32),
            V((group, 8, cols), f32),
            V((group, 8, cols), f32),
            V((2, 2, 8, cols), f32),
            V((2, rows, cols), f32),
            V((2, total + 16, cols), f32),
            V((total, 8, cols), f32),
            V((halves, total, GROUP, BLOCK), f32),
            V((halves, total, GROUP, BLOCK), f32),
            V((halves, total, GROUP, BLOCK), f32),
            V((WIDEST, 2, halves, GROUP, BLOCK), f32),
            V((halves, own, GROUP, BLOCK), f32),
            V((halves, max(rows - 2 * own, own), GROUP, BLOCK), f32),
            V((halves, own, GROUP, BLOCK), f32),
            V((chunks - 1, halves, rows, GROUP, BLOCK), f32),
            V((halves, own, species, BLOCK), f32),
            V((blocks, species, BLOCK), f32),
            V((species, reactions), i32),
            V((reactions, species), i32),
            V(log_rate.shape, f32),
            V((reactions, 2 * species), bf16),
            V((2 * species, 2 * reactions), bf16),
            V((log_rate.shape[0], reactions, BLOCK), f32),
            V((species, 2 * BLOCK), f32),
            V((species, 2 * BLOCK), f32),
            V((2 * species, 2 * BLOCK), bf16),
            V((2 * reactions, 2 * BLOCK), bf16),
            V((reactions, 2 * BLOCK), f32),
            D((2,)), D((3,)), D((2,)), D((2,)),
            D((2, 2)), D((2, 2)), D((2, 2)), D((2, 2)),
            D((n,)), D((n,)), D((n,)), D((n,)), D((n,)), D((n,)), D((n,)),
        ],
        compiler_params=pltpu.CompilerParams(
            collective_id=0, has_side_effects=True, vmem_limit_bytes=45 << 20
        ),
    )(conc, diffusion, *whole, facts, place)


def assemble_kernel(place, home, out, sems, *lines):
    group, rows, cols = out.shape
    halves, each = cols // BLOCK, lines[0].shape[0]
    own = rows // home.shape[0]

    def put(q, i, v):
        row = pl.multiple_of((q * each + i) * 8, 8)
        dst = out.at[:, pl.ds(row, 8), pl.ds(v * BLOCK, BLOCK)]
        return pltpu.make_async_copy(lines[q].at[i, v], dst, sems.at[q, i, v])

    for q in range(len(lines)):

        def fill(i, carry):
            at = (q * each + i) * 8
            source, row = lax.div(at, own), lax.rem(at, own)
            for v in range(halves):
                flat = lines[q].at[i, v].reshape(group * 8, BLOCK)
                where = [place[source, 0, (row + j) * halves + v] for j in range(8)]
                for g in range(0, group, 8):
                    for j in range(8):
                        flat[pl.ds(g * 8 + j, 8, stride=8), :] = home[source, where[j], g : g + 8, :]
            return carry

        lax.fori_loop(0, each, fill, 0)
        for i in range(each):
            for v in range(halves):
                put(q, i, v).start()
    for q in range(len(lines)):
        for i in range(each):
            for v in range(halves):
                put(q, i, v).wait()


def assemble(places, home, shape):
    group, rows, cols = shape
    halves, steps = cols // BLOCK, rows // 8
    each = steps // QUARTERS
    return pl.pallas_call(
        assemble_kernel,
        name="assemble",
        in_specs=[pl.BlockSpec(memory_space=pltpu.SMEM), pl.BlockSpec(memory_space=pltpu.VMEM)],
        out_specs=pl.BlockSpec(memory_space=pl.ANY),
        out_shape=jax.ShapeDtypeStruct(shape, jnp.float32),
        scratch_shapes=[pltpu.SemaphoreType.DMA((QUARTERS, each, halves))]
        + [pltpu.VMEM((each, halves, group, 8, BLOCK), jnp.float32)] * QUARTERS,
        compiler_params=pltpu.CompilerParams(vmem_limit_bytes=24 << 20),
    )(places, home)


def per_device(conc, diffusion, courant_x, courant_y, log_rate, reactants, products, block_class, send_slot):
    blocks = send_slot.shape[0]
    number = jnp.arange(blocks, dtype=jnp.int32)
    key = number + jnp.where(send_slot >= 0, blocks, 0)
    place = jnp.sum((key[None, :] < key[:, None]).astype(jnp.int32), axis=1)
    kinds = jnp.stack([number, send_slot, block_class])
    facts = jnp.sum(jnp.where(place[None, :, None] == number[None, None, :], kinds[:, :, None], 0), axis=1).reshape(-1)
    place = jnp.broadcast_to(jnp.pad(place, (0, BLOCK - blocks))[None], (8, BLOCK))
    home, places = take_step(
        conc, diffusion, courant_x, courant_y, log_rate, reactants, products, facts, place, lax.axis_size("species")
    )
    return assemble(places, home, conc.shape)


def solution(mesh):
    in_specs = (
        P("species", "region", None),
        P("species"),
        P("region", None),
        P("region", None),
        P(),
        P(),
        P(),
        P(("region", "species")),
        P(("region", "species")),
    )
    out_specs = P("species", "region", None)
    return jax.shard_map(per_device, mesh=mesh, in_specs=in_specs, out_specs=out_specs, check_vma=False)
```

```python
import functools

import jax
import jax.numpy as jnp
from jax import lax
from jax.experimental import pallas as pl
from jax.experimental.pallas import tpu as pltpu
from jax.sharding import PartitionSpec as P

STEPS = 3
ITERS = 2
SUB = 2
BLOCK = 128
FLOOR = 0.05
PAD = 8
GROUP = 8
WIDEST = 20
PIECES = 8
MESH = pl.DeviceIdType.MESH


def median0(p, r):
    return jnp.maximum(jnp.minimum(p, r), jnp.minimum(jnp.maximum(p, r), 0.0))


def next_column(vs, lane):
    r = [pltpu.roll(v, BLOCK - 1, 1) for v in vs] + [jnp.zeros_like(vs[0])]
    return [jnp.where(lane == BLOCK - 1, r[i + 1], r[i]) for i in range(len(vs))]


def previous_column(vs, lane):
    r = [jnp.zeros_like(vs[0])] + [pltpu.roll(v, 1, 1) for v in vs]
    return [jnp.where(lane == 0, r[i], r[i + 1]) for i in range(len(vs))]


def substep(src, dst, coef, nu, ahead, lo, groups, size, at):
    R = range(src.shape[0])
    lane = lax.broadcasted_iota(jnp.int32, (8, BLOCK), 1)

    def ld(e):
        return [src[v, e] for v in R]

    def c(e, k):
        whole = coef[e, pl.ds(k, 8, stride=0), :]
        return [whole[:, v * BLOCK : (v + 1) * BLOCK] for v in R]

    def right(e, k, q, s):
        a, b = c(e, k), c(e, k + 1)
        return [(a[v] + nu) * q[v] + b[v] * s[v] for v in R]

    def left(e, k, q, s):
        a, b = c(e, k), c(e, k + 1)
        return [(a[v] - nu) * q[v] + b[v] * s[v] for v in R]

    def minus(x, y):
        return [x[v] - y[v] for v in R]

    def plus(x, y):
        return [x[v] + y[v] for v in R]

    def slope(x, y):
        return [median0(x[v], y[v]) for v in R]

    def xstart(e):
        qb, qa, q0, q1 = ld(e - 2), ld(e - 1), ld(e), ld(e + 1)
        db, da, d0 = minus(qa, qb), minus(q0, qa), minus(q1, q0)
        sa, s0 = slope(db, da), slope(da, d0)
        f = plus(right(e - 1, 0, qa, sa), left(e, 2, q0, s0))
        return f, right(e, 0, q0, s0), d0, q1

    def xrow(e, carry):
        prev, out, d, q1 = carry
        q2 = ld(e + 2)
        d1 = minus(q2, q1)
        s = slope(d, d1)
        f = plus(out, left(e + 1, 2, q1, s))
        return minus(f, prev), (f, right(e + 1, 0, q1, s), d1, q2)

    def shift(t):
        for u in range(size):
            q = ld(lo + t * size + u)
            up, down = next_column(q, lane), previous_column(q, lane)
            for v in R:
                ahead[u, 0, v] = up[v]
                ahead[u, 1, v] = down[v]

    def update(t, carry):
        made = []
        for u in range(size):
            e = lo + t * size + u
            q = ld(e)
            up = [ahead[u, 0, v] for v in R]
            down = [ahead[u, 1, v] for v in R]
            s = slope(minus(q, down), minus(up, q))
            a, b = right(e, 4, q, s), left(e, 6, q, s)
            bn, ap = next_column(b, lane), previous_column(a, lane)
            div, carry = xrow(e, carry)
            made.append(minus(minus(minus(q, div), minus(a, b)), minus(bn, ap)))
        return made, carry

    def put(t, made):
        for u in range(size):
            for v in R:
                dst[v, at + t * size + u] = made[u][v]

    shift(0)

    def body(t, carry):
        made, carry = update(t - 1, carry)
        shift(t)
        put(t - 1, made)
        return carry

    carry = lax.fori_loop(1, groups, body, xstart(lo))
    made, _ = update(groups - 1, carry)
    put(groups - 1, made)


def next_lane(x, lane, cols):
    return jnp.where(lane == cols - 1, 0.0, pltpu.roll(x, cols - 1, 1))


def previous_lane(x, lane):
    return jnp.where(lane == 0, 0.0, pltpu.roll(x, 1, 1))


def face_coefficients(w, coef, starts):
    cols = w.shape[2]
    lane = lax.broadcasted_iota(jnp.int32, (8, cols), 1)

    def ahead(a):
        p = jnp.maximum(a, 0.0)
        return [p, p * (0.5 * (1.0 - a))]

    def behind(a):
        m = jnp.minimum(a, 0.0)
        return [m, m * (-0.5 * (1.0 + a))]

    for e in starts:
        before, here, after = [w[0, e + 8 + k : e + 16 + k, :] for k in (-1, 0, 1)]
        cy = w[1, e + 8 : e + 16, :]
        ax, bx = 0.5 * (here + after), 0.5 * (before + here)
        ay, by = 0.5 * (cy + next_lane(cy, lane, cols)), 0.5 * (cy + previous_lane(cy, lane))
        kinds = jnp.stack(ahead(ax) + behind(bx) + ahead(ay) + behind(by), axis=0)
        coef[e : e + 8] = jnp.swapaxes(kinds, 0, 1)


def split(m):
    size = max(k for k in range(1, WIDEST + 1) if m % k == 0)
    return m // size, size


def step_kernel(
    conc, nus, cx, cy, log_rate, reactants, products, facts, tile,
    home, places,
    xin, top, bottom, winds, courant, w, coef, buf, other, third, ahead, low, crossing, staying, high, made, gathered, done,
    reacts, makes, rates, first, second, logs, anchor, state, lifted, rated, kept,
    x_sem, t_sem, c_sem, l_sem, halo_s, halo_r, wind_s, wind_r, first_s, out_s, out_r, home_s, home_r, place_s, place_r,
):
    n, nr = lax.axis_size("species"), lax.axis_size("region")
    me, region = lax.axis_index("species"), lax.axis_index("region")
    group, rows, cols = conc.shape
    halves = cols // BLOCK
    own = rows // n
    total = rows + 2 * PAD
    chunks = group // GROUP
    species = group * n
    reactions = log_rate.shape[1]
    blocks = own * halves
    not_first, not_last = region > 0, region < nr - 1

    def peer(j):
        up = 2 * me < n
        t = jnp.where(up, n - 1 - j - (n - 1 - j <= me).astype(jnp.int32), j + (j >= me).astype(jnp.int32))
        return t, lax.rem(t - me + n, n)

    def fetch(c):
        slot = lax.rem(c, 2)
        return pltpu.make_async_copy(conc.at[pl.ds(c * GROUP, GROUP)], xin.at[slot], x_sem.at[slot])

    def remote(src, dst, send, recv, where):
        return pltpu.make_async_remote_copy(
            src_ref=src, dst_ref=dst, send_sem=send, recv_sem=recv, device_id=where, device_id_type=MESH
        )

    barrier = pltpu.get_barrier_semaphore()
    for s in range(1, n):
        pl.semaphore_signal(barrier, inc=1, device_id={"species": lax.rem(me + s, n)}, device_id_type=MESH)

    @pl.when(not_first)
    def _():
        pl.semaphore_signal(barrier, inc=1, device_id={"region": region - 1}, device_id_type=MESH)

    @pl.when(not_last)
    def _():
        pl.semaphore_signal(barrier, inc=1, device_id={"region": region + 1}, device_id_type=MESH)

    fetch(0).start()
    take_courant = [pltpu.make_async_copy(c, courant.at[k], c_sem.at[k]) for k, c in enumerate((cx, cy))]
    take_small = [
        pltpu.make_async_copy(a, b, t_sem.at[k])
        for k, (a, b) in enumerate(
            [(log_rate, rates), (reactants, reacts), (products, makes)]
        )
    ]
    for copy in take_courant + take_small:
        copy.start()
    for at in (0, PAD + 8 + rows):
        w[:, at : at + PAD + 8, :] = jnp.zeros((2, PAD + 8, cols), jnp.float32)

    @pl.when(region == 0)
    def _():
        top[...] = jnp.zeros_like(top)

    @pl.when(region == nr - 1)
    def _():
        bottom[...] = jnp.zeros_like(bottom)

    for copy in take_courant:
        copy.wait()
    w[:, PAD + 8 : PAD + 8 + rows, :] = courant[...]
    every = range(0, total, 8)
    inside = [e for e in every if e + 8 > PAD + own - 5 and e <= PAD + rows - own + 5]
    edge = [e for e in every if e not in inside or e in (0, 8, total - 16, total - 8)]
    face_coefficients(w, coef, inside)
    pl.semaphore_wait(barrier, n - 1 + not_first.astype(jnp.int32) + not_last.astype(jnp.int32))

    ends = [(0, GROUP), (GROUP, group - GROUP)]

    def wind_copy(d, k):
        c = (cx, cy)[k]
        src = c.at[pl.ds(rows - 8, 8)] if d == 0 else c.at[pl.ds(0, 8)]
        to = region + 1 if d == 0 else region - 1
        return remote(src, winds.at[d, k], wind_s.at[d, k], wind_r.at[d, k], {"region": to})

    def halo_copy(d, piece):
        at, size = ends[piece]
        src = conc.at[pl.ds(at, size), pl.ds(rows - 8 if d == 0 else 0, 8)]
        dst = (top, bottom)[d].at[pl.ds(at, size)]
        to = region + 1 if d == 0 else region - 1
        return remote(src, dst, halo_s.at[d, piece], halo_r.at[d, piece], {"region": to})

    def send_edges(d):
        for k in range(2):
            wind_copy(d, k).start()
        for piece in range(2):
            halo_copy(d, piece).start()

    pl.when(not_last)(lambda: send_edges(0))
    pl.when(not_first)(lambda: send_edges(1))

    def place_copy(t, s, source):
        return remote(tile, places.at[source], place_s.at[s], place_r.at[s], {"species": t})

    for j in range(n - 1):
        t, s = peer(j)
        place_copy(t, s, me).start()
    place_own = pltpu.make_async_copy(tile, places.at[me], l_sem.at[0])
    place_own.start()

    def take_winds(d):
        for k in range(2):
            wind_copy(d, k).wait_recv()
            at = 8 if d == 0 else 8 + PAD + rows
            w[k, at : at + 8, :] = winds[d, k]

    def clip(b):
        zeros = jnp.zeros((halves, PAD, GROUP, BLOCK), jnp.float32)

        @pl.when(region == 0)
        def _():
            b[:, 0:PAD] = zeros

        @pl.when(region == nr - 1)
        def _():
            b[:, PAD + rows : total] = zeros

    def take_halo(piece):
        pl.when(not_first)(lambda: halo_copy(0, piece).wait_recv())
        pl.when(not_last)(lambda: halo_copy(1, piece).wait_recv())

    def turn(value, at):
        moved = jnp.swapaxes(value, 0, 1)
        for v in range(halves):
            buf[v, pl.ds(at, 8)] = moved[:, :, v * BLOCK : (v + 1) * BLOCK]

    def out_copy(c, src, send, t, s):
        dst = gathered.at[:, :, pl.ds(me * group + c * GROUP, GROUP), :]
        return remote(src, dst, send.at[s], out_r.at[s], {"species": t})

    def arrive(c, start, groups):
        fetch(c).wait()

        @pl.when(c + 1 < chunks)
        def _():
            fetch(c + 1).start()

        turn_rows(c, start, groups)

    def turn_rows(c, start, groups):
        slot = lax.rem(c, 2)

        def inner(g, carry):
            r = pl.multiple_of(start + g * 8, 8)
            turn(xin[slot, :, pl.ds(r, 8), :], PAD + r)
            return carry

        lax.fori_loop(0, groups, inner, 0)

    def arrive_halo(c):
        at = pl.multiple_of(c * GROUP, GROUP)
        turn(top[pl.ds(at, GROUP)], 0)
        turn(bottom[pl.ds(at, GROUP)], PAD + rows)

    def spread(c):
        sub = lax.broadcasted_iota(jnp.int32, (GROUP, BLOCK), 0)
        nu = jnp.zeros((GROUP, BLOCK), jnp.float32)
        for k in range(GROUP):
            nu = jnp.where(sub == k, nus[c * GROUP + k], nu)
        return nu

    def advance(dst, nu, lo, size, mid, edge):
        wide, few = split(size + 8), split(size)
        substep(buf, other, coef, nu, ahead, PAD + lo - 4, *wide, PAD + lo - 4)
        if edge:
            clip(other)
        substep(other, mid, coef, nu, ahead, PAD + lo - 4, *wide, PAD + lo - 4)
        if edge:
            clip(mid)
        substep(mid, dst, coef, nu, ahead, PAD + lo, *few, 0)

    def keep(c, src, row):
        mine = pl.ds(pl.multiple_of(me * group + c * GROUP, GROUP), GROUP)
        for v in range(halves):
            gathered[v, :, mine, :] = src[v, pl.ds(row, own)]

    def strip(src, lo, size):
        def holds(t):
            return (t * own >= lo) & (t * own < lo + size)

        for j in range(n - 1):
            t, s = peer(j)

            @pl.when(holds(t))
            def _():
                out_copy(0, src.at[:, pl.ds(t * own - lo, own)], first_s, t, s).start()

        @pl.when(holds(me))
        def _():
            keep(0, src, me * own - lo)

    nu = spread(0)
    size = rows // 2 - own
    if size > 0:
        upper = 2 * me < n
        one, two = jnp.where(upper, rows // 2, own), jnp.where(upper, own, rows // 2)
        arrive(0, one - 8, (size + 16) // 8)
        advance(crossing, nu, one, size, third, False)
        strip(crossing, one, size)
        turn_rows(0, 0, rows // 8)
        advance(staying, nu, two, size, third, False)
        strip(staying, two, size)
    else:
        arrive(0, 0, rows // 8)
    pl.when(not_first)(lambda: take_winds(0))
    pl.when(not_last)(lambda: take_winds(1))
    face_coefficients(w, coef, edge)
    take_halo(0)
    arrive_halo(0)
    advance(low, nu, 0, own, third, True)
    strip(low, 0, own)
    advance(high, nu, rows - own, own, third, True)
    strip(high, rows - own, own)
    take_halo(1)

    def chunk(c, carry):
        arrive(c, 0, rows // 8)
        arrive_halo(c)
        advance(made.at[c - 1], spread(c), 0, rows, buf, True)
        for j in range(n - 1):
            t, s = peer(j)
            out_copy(c, made.at[c - 1, :, pl.ds(t * own, own)], out_s, t, s).start()
        keep(c, made.at[c - 1], me * own)
        return carry

    lax.fori_loop(1, chunks, chunk, 0)

    for copy in take_small:
        copy.wait()
    for i in range(0, species, BLOCK):
        for j in range(0, reactions, BLOCK):
            ii, jj = slice(i, i + BLOCK), slice(j, j + BLOCK)
            uses = reacts[ii, jj].astype(jnp.float32)
            gives = makes[jj, ii].astype(jnp.float32)
            used, given = uses.T.astype(jnp.bfloat16), gives.T.astype(jnp.bfloat16)
            uses = uses.astype(jnp.bfloat16)
            first[jj, ii] = used
            first[jj, species + i : species + i + BLOCK] = used
            second[ii, jj] = given
            second[ii, reactions + j : reactions + j + BLOCK] = given
            second[species + i : species + i + BLOCK, jj] = uses
            second[species + i : species + i + BLOCK, reactions + j : reactions + j + BLOCK] = uses
    for k in range(log_rate.shape[0]):
        for j in range(0, reactions, BLOCK):
            row = jnp.broadcast_to(rates[k : k + 1, j : j + BLOCK], (BLOCK, BLOCK))
            logs[k, j : j + BLOCK, :] = row.T

    for s in range(1, n):
        source = lax.rem(me - s + n, n)
        part = gathered.at[:, :, pl.ds(source * group, group), :]
        remote(part, part, out_s.at[s], out_r.at[s], {"species": source}).wait_recv()

    lane = lax.broadcasted_iota(jnp.int32, (1, 2 * BLOCK), 1)

    def iterate(stride):
        lg = jnp.log(state[...])
        hi = lg.astype(jnp.bfloat16)
        lifted[:species] = hi
        lifted[species:] = (lg - hi.astype(jnp.float32)).astype(jnp.bfloat16)
        summed = jnp.dot(first[...], lifted[...], preferred_element_type=jnp.float32)
        rate = jnp.exp(kept[...] + summed)
        hi = rate.astype(jnp.bfloat16)
        rated[:reactions] = hi
        rated[reactions:] = (rate - hi.astype(jnp.float32)).astype(jnp.bfloat16)
        both = jnp.dot(second[...], rated[...], preferred_element_type=jnp.float32)
        state[...] = (anchor[...] + stride * both[:species]) / (1.0 + stride * both[species:] / state[...])

    slow = (blocks - min(nr, blocks)) // 2

    def home_copy(p, t, s):
        return remote(
            done.at[pl.ds(2 * p, 2), pl.ds(t * group, group), :],
            home.at[me, pl.ds(2 * p, 2)],
            home_s.at[s], home_r.at[s], {"species": t},
        )

    def pair(p, carry):
        where = [facts[2 * p], facts[2 * p + 1]]
        stiff = [facts[blocks + 2 * p + k] >= 0 for k in range(2)]
        for k in range(2):
            lanes = slice(k * BLOCK, (k + 1) * BLOCK)
            b = where[k]
            value = jnp.maximum(gathered[lax.rem(b, halves), lax.div(b, halves)], FLOOR)
            anchor[:, lanes] = value
            state[:, lanes] = value
            kept[:, lanes] = logs[facts[2 * blocks + 2 * p + k]]

        def again_from(u, carry):
            other_stride = jnp.where(u == 0, 1.0, 0.0)
            left, right = [jnp.where(f, 1.0 / SUB, other_stride) for f in stiff]
            stride = jnp.where(lane < BLOCK, left, right)

            @pl.when(u > 0)
            def _():
                anchor[...] = state[...]

            def again(_, carry):
                iterate(stride)
                return carry

            return lax.fori_loop(0, ITERS, again, carry)

        lax.fori_loop(0, jnp.where(p >= slow, SUB, 1), again_from, 0)
        for k in range(2):
            done[2 * p + k] = state[:, k * BLOCK : (k + 1) * BLOCK]
        for j in range(n - 1):
            t, s = peer(j)
            home_copy(p, t, s).start()
        return carry

    lax.fori_loop(0, blocks // 2, pair, 0)
    kept_home = pltpu.make_async_copy(done.at[:, pl.ds(me * group, group), :], home.at[me], l_sem.at[1])
    kept_home.start()

    def edges_sent(d):
        for k in range(2):
            wind_copy(d, k).wait_send()
        for piece in range(2):
            halo_copy(d, piece).wait_send()

    pl.when(not_last)(lambda: edges_sent(0))
    pl.when(not_first)(lambda: edges_sent(1))
    place_own.wait()
    kept_home.wait()
    for s in range(1, n):
        t, source = lax.rem(me + s, n), lax.rem(me - s + n, n)
        place_copy(t, s, me).wait_send()
        place_copy(t, s, source).wait_recv()
        remote(low, low, first_s.at[s], out_r.at[s], {"species": t}).wait_send()
        sent = made.at[:, :, pl.ds(t * own, own)]
        remote(sent, sent, out_s.at[s], out_r.at[s], {"species": t}).wait_send()
        sent = done.at[:, pl.ds(t * group, group), :]
        remote(sent, home.at[me], home_s.at[s], home_r.at[s], {"species": t}).wait_send()
        remote(sent, home.at[source], home_s.at[s], home_r.at[s], {"species": t}).wait_recv()


def take_step(conc, diffusion, courant_x, courant_y, log_rate, reactants, products, facts, place, n):
    group, rows, cols = conc.shape
    halves, own = cols // BLOCK, rows // n
    species, reactions = reactants.shape
    chunks, blocks = group // GROUP, own * halves
    total = rows + 2 * PAD
    f32, bf16, i32 = jnp.float32, jnp.bfloat16, jnp.int32
    V, D = pltpu.VMEM, pltpu.SemaphoreType.DMA
    whole = [pltpu.with_memory_space_constraint(a, pltpu.HBM) for a in (courant_x, courant_y, log_rate, reactants, products)]
    hbm, smem = pl.BlockSpec(memory_space=pltpu.HBM), pl.BlockSpec(memory_space=pltpu.SMEM)
    return pl.pallas_call(
        step_kernel,
        name="step",
        in_specs=[hbm, smem] + [hbm] * 5 + [smem, pl.BlockSpec(memory_space=pltpu.VMEM)],
        out_specs=[pl.BlockSpec(memory_space=pl.ANY)] * 2,
        out_shape=[
            jax.ShapeDtypeStruct((n, blocks, group, BLOCK), f32),
            jax.ShapeDtypeStruct((n, 8, BLOCK), i32),
        ],
        scratch_shapes=[
            V((2, GROUP, rows, cols), f32),
            V((group, 8, cols), f32),
            V((group, 8, cols), f32),
            V((2, 2, 8, cols), f32),
            V((2, rows, cols), f32),
            V((2, total + 16, cols), f32),
            V((total, 8, cols), f32),
            V((halves, total, GROUP, BLOCK), f32),
            V((halves, total, GROUP, BLOCK), f32),
            V((halves, total, GROUP, BLOCK), f32),
            V((WIDEST, 2, halves, GROUP, BLOCK), f32),
            V((halves, own, GROUP, BLOCK), f32),
            V((halves, max(rows // 2 - own, own), GROUP, BLOCK), f32),
            V((halves, max(rows // 2 - own, own), GROUP, BLOCK), f32),
            V((halves, own, GROUP, BLOCK), f32),
            V((chunks - 1, halves, rows, GROUP, BLOCK), f32),
            V((halves, own, species, BLOCK), f32),
            V((blocks, species, BLOCK), f32),
            V((species, reactions), i32),
            V((reactions, species), i32),
            V(log_rate.shape, f32),
            V((reactions, 2 * species), bf16),
            V((2 * species, 2 * reactions), bf16),
            V((log_rate.shape[0], reactions, BLOCK), f32),
            V((species, 2 * BLOCK), f32),
            V((species, 2 * BLOCK), f32),
            V((2 * species, 2 * BLOCK), bf16),
            V((2 * reactions, 2 * BLOCK), bf16),
            V((reactions, 2 * BLOCK), f32),
            D((2,)), D((3,)), D((2,)), D((2,)),
            D((2, 2)), D((2, 2)), D((2, 2)), D((2, 2)),
            D((n,)), D((n,)), D((n,)), D((n,)), D((n,)), D((n,)), D((n,)),
        ],
        compiler_params=pltpu.CompilerParams(
            collective_id=0, has_side_effects=True, vmem_limit_bytes=45 << 20
        ),
    )(conc, diffusion, *whole, facts, place)


def assemble_kernel(place, home, out, sems, *lines):
    group, rows, cols = out.shape
    halves, each = cols // BLOCK, lines[0].shape[0]
    own = rows // home.shape[0]

    def put(q, i, v):
        row = pl.multiple_of((q * each + i) * 8, 8)
        dst = out.at[:, pl.ds(row, 8), pl.ds(v * BLOCK, BLOCK)]
        return pltpu.make_async_copy(lines[q].at[i, v], dst, sems.at[q, i, v])

    for q in range(len(lines)):

        def fill(i, carry):
            at = (q * each + i) * 8
            source, row = lax.div(at, own), lax.rem(at, own)
            for v in range(halves):
                flat = lines[q].at[i, v].reshape(group * 8, BLOCK)
                where = [place[source, 0, (row + j) * halves + v] for j in range(8)]
                for g in range(0, group, 8):
                    for j in range(8):
                        flat[pl.ds(g * 8 + j, 8, stride=8), :] = home[source, where[j], g : g + 8, :]
            return carry

        lax.fori_loop(0, each, fill, 0)
        for i in range(each):
            for v in range(halves):
                put(q, i, v).start()
    for q in range(len(lines)):
        for i in range(each):
            for v in range(halves):
                put(q, i, v).wait()


def assemble(places, home, shape):
    group, rows, cols = shape
    halves, steps = cols // BLOCK, rows // 8
    each = steps // PIECES
    return pl.pallas_call(
        assemble_kernel,
        name="assemble",
        in_specs=[pl.BlockSpec(memory_space=pltpu.SMEM), pl.BlockSpec(memory_space=pltpu.VMEM)],
        out_specs=pl.BlockSpec(memory_space=pl.ANY),
        out_shape=jax.ShapeDtypeStruct(shape, jnp.float32),
        scratch_shapes=[pltpu.SemaphoreType.DMA((PIECES, each, halves))]
        + [pltpu.VMEM((each, halves, group, 8, BLOCK), jnp.float32)] * PIECES,
        compiler_params=pltpu.CompilerParams(vmem_limit_bytes=24 << 20),
    )(places, home)


def per_device(conc, diffusion, courant_x, courant_y, log_rate, reactants, products, block_class, send_slot):
    blocks = send_slot.shape[0]
    number = jnp.arange(blocks, dtype=jnp.int32)
    key = number + jnp.where(send_slot >= 0, blocks, 0)
    place = jnp.sum((key[None, :] < key[:, None]).astype(jnp.int32), axis=1)
    kinds = jnp.stack([number, send_slot, block_class])
    facts = jnp.sum(jnp.where(place[None, :, None] == number[None, None, :], kinds[:, :, None], 0), axis=1).reshape(-1)
    place = jnp.broadcast_to(jnp.pad(place, (0, BLOCK - blocks))[None], (8, BLOCK))
    home, places = take_step(
        conc, diffusion, courant_x, courant_y, log_rate, reactants, products, facts, place, lax.axis_size("species")
    )
    return assemble(places, home, conc.shape)


def solution(mesh):
    in_specs = (
        P("species", "region", None),
        P("species"),
        P("region", None),
        P("region", None),
        P(),
        P(),
        P(),
        P(("region", "species")),
        P(("region", "species")),
    )
    out_specs = P("species", "region", None)
    return jax.shard_map(per_device, mesh=mesh, in_specs=in_specs, out_specs=out_specs, check_vma=False)
```
